256 devices in a mesh: prow: 16 (over z, core), pcol: 16 (over y, x).
Axes of the slice: x: 4, y: 4, z: 8, core: 2. Of those that a mesh axis runs over, the one named last changes fastest.
Arguments:
- root_inverse: float32 [2, 16, 128, 2, 16, 128], P(None, 'prow', None, None, 'pcol'), as said below
- lower_one: float32 [2, 16, 128, 1, 16, 128], P(None, 'prow', None, None, 'pcol'), may hold values from -0.125 to 0.125
- lower_two: float32 [3, 16, 128, 1, 16, 128], P(None, 'prow', None, None, 'pcol'), may hold values from -0.15625 to 0.15625
- dinv_one: float32 [1, 16, 128, 1, 16, 128], P(None, 'prow', None, None, 'pcol'), as said below
- dinv_two: float32 [1, 16, 128, 1, 16, 128], P(None, 'prow', None, None, 'pcol'), as said below
- seg_one: int32 [16], replicated, may hold values from 0 to 2, as said below
- seg_two: int32 [16], replicated, may hold values from 0 to 3, as said below
- parent_two: int32 [4], replicated, may hold values from 0 to 2
- pattern_one: int32 [3, 32], replicated, may hold values 0 or 1
- pattern_two: int32 [4, 48], replicated, may hold values 0 or 1
Outputs:
- inverse_one: float32 [1, 16, 128, 1, 16, 128], P(None, 'prow', None, None, 'pcol')
- inverse_two: float32 [1, 16, 128, 1, 16, 128], P(None, 'prow', None, None, 'pcol')
The draws below stay inside these ranges and needn't reach their ends.
Inputs may be any that keep to these rules, and one draw needn't show every extreme that they name: `root_inverse`: Block-diagonal over supernodes is not implied; this is a symmetric matrix. `dinv_one`: Symmetric, and zero in every block whose row and column blocks belong to different supernodes of seg_one. `dinv_two`: Symmetric, and zero in every block whose row and column blocks belong to different supernodes of seg_two. `seg_one`: never falls; every supernode 0 to 2 has 1 to 8 consecutive blocks, one exactly 8. `seg_two`: never falls; every supernode 0 to 3 has 1 to 8 consecutive blocks, one exactly 8.
All inputs are finite; a program needn't handle non-finite values.
Results may differ from the reference program's by a relative error of at most 0.00005.
Values sent between devices are 32-bit elements; how exact they have to be, the bound alone decides.
A program may use at most 64 MiB of HBM per device.

```python
import math
import jax
import jax.numpy as jnp
from jax import lax

B = 128
NR = 32
W1 = 16
W2 = 16
C1 = 3
C2 = 4
R2 = 48
N_PROW = 16
N_PCOL = 16


def segment_ids(key, block_total, supernodes):
    biggest = block_total // 2
    remainder = block_total - biggest
    where_big = jax.random.randint(jax.random.fold_in(key, 1), (), 0, supernodes)
    shuffled = jax.random.permutation(jax.random.fold_in(key, 2), remainder - 1) + 1
    cut_points = jnp.sort(shuffled[:supernodes - 2]).astype(jnp.int32)
    bounds = jnp.concatenate([jnp.zeros((1,), jnp.int32), cut_points, jnp.full((1,), remainder, jnp.int32)])
    smaller = bounds[1:] - bounds[:-1]
    padded = jnp.concatenate([smaller, jnp.zeros((1,), jnp.int32)])
    shifted = jnp.concatenate([jnp.zeros((1,), jnp.int32), smaller])
    position = jnp.arange(supernodes, dtype=jnp.int32)
    sizes_all = jnp.where(position < where_big, padded, jnp.where(position == where_big, biggest, shifted))
    endings = jnp.cumsum(sizes_all)
    block_ids = jnp.arange(block_total, dtype=jnp.int32)
    return jnp.sum((block_ids[:, None] >= endings[None, :]).astype(jnp.int32), axis=1).astype(jnp.int32)


def symmetric_body(key, order, spread):
    raw_values = jax.random.normal(jax.random.fold_in(key, 3), (order, order), jnp.float32)
    diagonal = 1.0 + jax.random.uniform(jax.random.fold_in(key, 4), (order,), jnp.float32, 0.0, 1.0)
    off_part = (raw_values + raw_values.T) * 0.5 * spread
    return off_part + jnp.diag(diagonal)


def supernode_inverse(key, block_total, seg_ids):
    order = block_total * B
    matrix = symmetric_body(key, order, 0.6 / math.sqrt(block_total // 2 * B))
    member = seg_ids[jnp.arange(order, dtype=jnp.int32) // B]
    same_node = member[:, None] == member[None, :]
    kept = jnp.where(same_node, matrix, 0.0).astype(jnp.float32)
    return kept.reshape(block_total // N_PROW, N_PROW, B, block_total // N_PCOL, N_PCOL, B)


def draw_root_inverse(key, part):
    order = NR * B
    matrix = symmetric_body(jax.random.fold_in(key, 31), order, 0.6 / math.sqrt(order))
    return matrix.astype(jnp.float32).reshape(NR // N_PROW, N_PROW, B, NR // N_PCOL, N_PCOL, B)


def draw_seg_one(key, part):
    return segment_ids(jax.random.fold_in(key, 11), W1, C1)


def draw_dinv_one(key, part):
    seg_ids = segment_ids(jax.random.fold_in(key, 11), W1, C1)
    return supernode_inverse(jax.random.fold_in(key, 12), W1, seg_ids)


def draw_seg_two(key, part):
    return segment_ids(jax.random.fold_in(key, 21), W2, C2)


def draw_dinv_two(key, part):
    seg_ids = segment_ids(jax.random.fold_in(key, 21), W2, C2)
    return supernode_inverse(jax.random.fold_in(key, 22), W2, seg_ids)


def with_ends(drawn, key, smallest, high):
    index_at = [jax.random.randint(jax.random.fold_in(key, axis), (), 0, length) for axis, length in enumerate(drawn.shape)]
    longest = drawn.shape.index(max(drawn.shape))
    neighbour = index_at[:longest] + [(index_at[longest] + 1) % drawn.shape[longest]] + index_at[longest + 1:]
    return drawn.at[tuple(index_at)].set(smallest).at[tuple(neighbour)].set(high)


def level_of(own_key, extent, shards, low, high):
    factor_of, own = 1.0, jax.random.fold_in(own_key, 6)
    for axis_at, shards_of in shards:
        steps = jnp.exp(jax.random.uniform(jax.random.fold_in(own, axis_at), (shards_of,), jnp.float32, low / len(shards), high / len(shards)))
        factor_of = factor_of * jnp.repeat(steps, extent[axis_at] // shards_of).reshape([-1 if axis == axis_at else 1 for axis in range(len(extent))])
    return factor_of


def gaussian(key, shape, deviation, bound, cuts=(), kind=jnp.bfloat16):
    factor_of = level_of(key, shape, cuts, -0.22, 0.18) if cuts else 1.0
    entries = jax.random.normal(key, shape, jnp.float32) * deviation * factor_of
    return jnp.minimum(jnp.maximum(entries, -bound), bound).astype(kind)


def setup_inputs(seed: int = 0) -> dict:
    splits = jax.random.split(jax.random.key(seed), 11)
    return {
        "root_inverse": draw_root_inverse(jax.random.fold_in(splits[10], 71), 0),
        "lower_one": gaussian(splits[1], (NR // N_PROW, N_PROW, B, W1 // N_PCOL, N_PCOL, B), (NR * B // 2) ** -0.5, 0.125, ((1, 16), (4, 16)), jnp.float32),
        "lower_two": gaussian(splits[2], (R2 // N_PROW, N_PROW, B, W2 // N_PCOL, N_PCOL, B), (R2 * B // 4) ** -0.5, 0.15625, ((1, 16), (4, 16)), jnp.float32),
        "dinv_one": draw_dinv_one(jax.random.fold_in(splits[10], 71), 0),
        "dinv_two": draw_dinv_two(jax.random.fold_in(splits[10], 71), 0),
        "seg_one": draw_seg_one(jax.random.fold_in(splits[10], 71), 0),
        "seg_two": draw_seg_two(jax.random.fold_in(splits[10], 71), 0),
        "parent_two": with_ends(jax.random.randint(splits[7], (C2,), 0, C1), jax.random.fold_in(splits[7], 1), 0, C1 - 1).astype(jnp.int32),
        "pattern_one": with_ends((jax.random.randint(splits[8], (C1, NR), 0, 2) < 1).astype(jnp.int32), jax.random.fold_in(splits[8], 1), 0, 1),
        "pattern_two": with_ends((jax.random.randint(splits[9], (C2, R2), 0, 2) < 1).astype(jnp.int32), jax.random.fold_in(splits[9], 1), 0, 1),
    }


def as_matrix(blocks):
    shape_now = blocks.shape
    return blocks.reshape(shape_now[0] * shape_now[1] * shape_now[2], shape_now[3] * shape_now[4] * shape_now[5])


def as_blocks(matrix, block_rows, block_cols):
    return matrix.reshape(block_rows // N_PROW, N_PROW, B, block_cols // N_PCOL, N_PCOL, B)


def expand(block_mask):
    return jnp.repeat(jnp.repeat(block_mask, B, axis=0), B, axis=1)


def product(left_side, right_side):
    return jnp.dot(left_side, right_side, precision=lax.Precision.HIGHEST, preferred_element_type=jnp.float32)


def reference(root_inverse, lower_one, lower_two, dinv_one, dinv_two, seg_one, seg_two, parent_two, pattern_one, pattern_two):
    root_matrix = as_matrix(root_inverse)
    mask_one = pattern_one[seg_one, :].T.astype(jnp.float32)
    masked_one = as_matrix(lower_one) * expand(mask_one)
    solved_one = product(root_matrix, masked_one)
    same_one = (seg_one[:, None] == seg_one[None, :]).astype(jnp.float32)
    inverse_one = (as_matrix(dinv_one) + product(masked_one.T, solved_one)) * expand(same_one)
    region = jnp.concatenate([
        jnp.concatenate([root_matrix, -solved_one], axis=1),
        jnp.concatenate([-solved_one.T, inverse_one], axis=1)], axis=0)
    parent_of = parent_two[seg_two]
    root_reach = pattern_one[parent_of, :]
    level_reach = (seg_one[None, :] == parent_of[:, None]).astype(jnp.int32)
    reachable = jnp.concatenate([root_reach, level_reach], axis=1)
    mask_two = (pattern_two[seg_two, :] * reachable).T.astype(jnp.float32)
    masked_two = as_matrix(lower_two) * expand(mask_two)
    solved_two = product(region, masked_two)
    same_two = (seg_two[:, None] == seg_two[None, :]).astype(jnp.float32)
    inverse_two = (as_matrix(dinv_two) + product(masked_two.T, solved_two)) * expand(same_two)
    return as_blocks(inverse_one, W1, W1), as_blocks(inverse_two, W2, W2)
```

```python
import jax
import jax.numpy as jnp
from jax import lax
from jax.experimental import pallas as pl
from jax.experimental.pallas import tpu as pltpu
from jax.sharding import PartitionSpec as P

MESH = pl.DeviceIdType.MESH
F32 = jnp.float32
BF16 = jnp.bfloat16
B = 128
NX = 4
NY = 4
NZ = 8
NB = 16

GATHER = 40
M_G1 = 0
M_GE = M_G1 + GATHER
M_BD = M_GE + GATHER
M_BZ = M_BD + GATHER
M_Y1 = M_BZ + 15
M_Y2 = M_Y1 + 15
M_Z1 = M_Y2 + 15
M_Z2 = M_Z1 + 15
M_T1 = M_Z2 + 15
M_T2 = M_T1 + 2
M_F1 = M_T2 + 2
M_F2 = M_F1 + 1
M_ALL = M_F2 + 1


def split(x):
    hi = x.astype(BF16)
    lo = (x - hi.astype(F32)).astype(BF16)
    return hi, lo


def left3(x):
    hi, lo = split(x)
    return jnp.concatenate([hi, hi, lo], axis=1)


def right3(x):
    hi, lo = split(x)
    return jnp.concatenate([hi, lo, hi], axis=0)


def dot(a, b):
    return jnp.dot(a, b, preferred_element_type=F32)


def rounds(*flows):
    flows = list(flows)
    while flows:
        for flow in list(flows):
            try:
                next(flow)
            except StopIteration:
                flows.remove(flow)


def kernel(
    seg1, seg2, par2, pat1, pat2,
    r_ref, l1_ref, l2_ref, d1_ref, d2_ref,
    o1_ref, o2_ref,
    g1, ge, gbd, bz,
    p1, x1, rp1, rm1,
    p2, x2, rp2, rm2,
    pz1, xz1, rpz1, rmz1,
    pz2, xz2, rpz2, rmz2,
    yt1, yt2, w1, w2, rw, ew,
    send, recv,
):
    p = lax.axis_index("prow")
    q = lax.axis_index("pcol")
    z = p // 2
    c = p % 2
    y = q // NX
    x = q % NX
    sibling = (2 * z + 1 - c, q)
    z_up = (2 * ((z + 1) % NZ) + c, q)
    z_down = (2 * ((z + NZ - 1) % NZ) + c, q)
    diagonal = p == q
    pending = []

    def remote(m, src, dst, device):
        return pltpu.make_async_remote_copy(
            src_ref=src,
            dst_ref=dst,
            send_sem=send.at[m],
            recv_sem=recv.at[m],
            device_id=device,
            device_id_type=MESH,
        )

    def push(m, src, dst, device):
        copy = remote(m, src, dst, device)
        copy.start()
        pending.append(copy)

    def arrive(m, dst):
        remote(m, dst, dst, sibling).wait_recv()

    s1 = seg1[q]
    s2 = seg2[q]
    parent = par2[s2]
    for a in range(2):
        m1 = pat1[s1, p + NB * a].astype(F32)
        g1[a, q] = (l1_ref[pl.ds(B * a, B), :] * m1).T
    mb = (pat2[s2, 2 * NB + p] * (seg1[p] == parent).astype(jnp.int32)).astype(F32)
    own_b = (l2_ref[pl.ds(2 * B, B), :] * mb).T
    bz[p] = own_b
    gbd[0, q] = own_b
    gbd[1, q] = d1_ref[...].T

    barrier = pltpu.get_barrier_semaphore()
    plane = [
        (p, y * NX + (x + 1) % NX),
        (p, y * NX + (x + NX - 1) % NX),
        (p, ((y + 1) % NY) * NX + x),
        (p, ((y + NY - 1) % NY) * NX + x),
    ]
    for device in plane + [sibling, z_up, z_down]:
        pl.semaphore_signal(barrier, inc=1, device_id=device, device_id_type=MESH)
    for i in range(2):
        source = 2 * (q // 2) + i

        @pl.when(jnp.logical_not(diagonal & (c == i)))
        def _():
            pl.semaphore_signal(barrier, inc=1, device_id=(source, p), device_id_type=MESH)

    pl.semaphore_wait(barrier, 9 - diagonal.astype(jnp.int32))

    def gather(g, base):
        top, low, whole = pl.ds(0, B // 2), pl.ds(B // 2, B // 2), pl.ds(0, B)

        class Half:
            pass

        halves = []
        for h in range(2):
            s = Half()
            s.h, s.base = h, base + 20 * h
            s.u, s.v = (x, y) if h == 0 else (y, x)
            halves.append(s)

        def slot(s, du, dv, rows):
            u, v = (s.u + du) % 4, (s.v + dv) % 4
            k = v * NX + u if s.h == 0 else u * NX + v
            return g.at[s.h, k, rows]

        def device(s, du, dv):
            u, v = (s.u + du) % 4, (s.v + dv) % 4
            return (p, v * NX + u if s.h == 0 else u * NX + v)

        def first(s, m, du, step, rows):
            view = slot(s, du, 0, rows)
            push(s.base + m, view, view, device(s, step, 0))

        def second(s, m, du, dv, step, rows):
            view = slot(s, du, dv, rows)
            push(s.base + m, view, view, device(s, 0, step))

        def spread(s, i, du):
            second(s, 4 + 2 * i, du, 0, 1, whole)
            second(s, 5 + 2 * i, du, 0, 3, whole)

        def pass_on(s, i, du):
            arrive(s.base + 4 + 2 * i, slot(s, du, 3, whole))
            second(s, 12 + 2 * i, du, 3, 1, top)
            arrive(s.base + 5 + 2 * i, slot(s, du, 1, whole))
            second(s, 13 + 2 * i, du, 1, 3, low)

        offsets = (0, 3, 1, 2)
        for s in halves:
            first(s, 0, 0, 1, whole)
            first(s, 1, 0, 3, whole)
        for s in halves:
            spread(s, 0, 0)
        yield
        for s in halves:
            arrive(s.base, slot(s, 3, 0, whole))
            first(s, 2, 3, 1, top)
            spread(s, 1, 3)
            arrive(s.base + 1, slot(s, 1, 0, whole))
            first(s, 3, 1, 3, low)
            spread(s, 2, 1)
        yield
        for s in halves:
            pass_on(s, 0, 0)
        yield
        for s in halves:
            arrive(s.base + 2, slot(s, 2, 0, top))
            arrive(s.base + 3, slot(s, 2, 0, low))
            spread(s, 3, 2)
        yield
        for i in (1, 2):
            for s in halves:
                pass_on(s, i, offsets[i])
        yield
        for s in halves:
            pass_on(s, 3, 2)
        yield
        for i in range(4):
            for s in halves:
                arrive(s.base + 12 + 2 * i, slot(s, offsets[i], 2, top))
                arrive(s.base + 13 + 2 * i, slot(s, offsets[i], 2, low))

    def column():
        def slot(dz, core):
            return bz.at[2 * ((z + dz + NZ) % NZ) + core]

        def send_to(m, dz, device):
            view = slot(dz, c)
            push(M_BZ + m, view, view, device)

        send_to(0, 0, z_up)
        send_to(4, 0, z_down)
        send_to(7, 0, sibling)
        yield
        for t in range(1, 5):
            arrive(M_BZ + t - 1, slot(-t, c))
            if t < 4:
                send_to(t, -t, z_up)
            send_to(7 + t, -t, sibling)
            if t < 4:
                arrive(M_BZ + 4 + t - 1, slot(t, c))
                if t < 3:
                    send_to(4 + t, t, z_down)
                send_to(11 + t, t, sibling)
            yield
        arrive(M_BZ + 7, slot(0, 1 - c))
        for t in range(1, 5):
            arrive(M_BZ + 7 + t, slot(-t, 1 - c))
            if t < 4:
                arrive(M_BZ + 11 + t, slot(t, 1 - c))

    def reduce(part, other, up, down, base):
        order = (4, -3, 3, -2, 2, -1, 1, 0)

        def pair(off):
            return pl.ds(2 * ((z + off + NZ) % NZ), 2)

        for n, off in enumerate(order):
            push(base + n, part.at[1 - c, pair(off)], other.at[pair(off)], sibling)
        yield

        def own(n):
            arrive(base + n, other.at[pair(order[n])])
            return part[c, pair(order[n])] + other[pair(order[n])]

        for t in range(4):
            n = 2 * t
            total = own(n)
            if t > 0:
                arrive(base + 8 + t - 1, up.at[t - 1])
                total = total + up[t - 1]
            part[c, pair(order[n])] = total
            push(base + 8 + t, part.at[c, pair(order[n])], up.at[t], z_up)
            if t < 3:
                n = 2 * t + 1
                total = own(n)
                if t > 0:
                    arrive(base + 12 + t - 1, down.at[t - 1])
                    total = total + down[t - 1]
                part[c, pair(order[n])] = total
                push(base + 12 + t, part.at[c, pair(order[n])], down.at[t], z_down)
            yield
        total = own(7)
        arrive(base + 14, down.at[2])
        total = total + down[2]
        arrive(base + 11, up.at[3])
        part[c, pair(0)] = total + up[3]

    def transpose_out(part, yt, base):
        for i in range(2):
            mine = part.at[c, 2 * z + i]
            copy = pltpu.make_async_remote_copy(
                src_ref=mine,
                dst_ref=yt.at[c],
                send_sem=send.at[base + i],
                recv_sem=recv.at[base + c],
                device_id=(q, 2 * z + i),
                device_id_type=MESH,
            )
            itself = diagonal & (c == i)

            @pl.when(itself)
            def _():
                yt[c] = part[c, 2 * z + i]

            @pl.when(jnp.logical_not(itself))
            def _():
                copy.start()

    def transpose_sent(part, yt, base):
        for i in range(2):
            @pl.when(jnp.logical_not(diagonal & (c == i)))
            def _():
                remote(base + i, part.at[c, 2 * z + i], yt.at[c], (q, 2 * z + i)).wait_send()

    def transpose_in(yt, base):
        for i in range(2):
            @pl.when(jnp.logical_not(diagonal & (c == i)))
            def _():
                arrive(base + i, yt.at[i])
        return right3(jnp.concatenate([yt[0].T, yt[1].T], axis=0))

    GROUP = 4

    def panel(g, i):
        rows = pl.ds(i * GROUP, GROUP)
        return jnp.concatenate(
            [g[0, rows].reshape(GROUP * B, B), g[1, rows].reshape(GROUP * B, B)], axis=1
        )

    def times_root(g, part):
        @pl.loop(0, NB // GROUP)
        def _(i):
            out = dot(left3(panel(g, i)), rw[...])
            rows = pl.ds(i * GROUP, GROUP)
            part[0, rows] = out[:, :B].reshape(GROUP, B, B)
            part[1, rows] = out[:, B:].reshape(GROUP, B, B)

    def store_halves(part, i, out):
        rows = pl.ds(i * GROUP, GROUP)
        blocks = out.reshape(GROUP, B, B)
        part[0, rows] = blocks[:, : B // 2]
        part[1, rows] = blocks[:, B // 2 :]

    def finish(part, w, base):
        push(base, part.at[c, 2 * z + 1 - c], w.at[c], sibling)
        w[c] = part[c, p]
        arrive(base, w.at[1 - c])

    rw[...] = right3(
        jnp.concatenate(
            [r_ref[pl.ds(0, 2 * B, stride=2), :], r_ref[pl.ds(1, 2 * B, stride=2), :]], axis=1
        )
    )

    rounds(gather(g1, M_G1), column())

    for a in range(2):
        ma = (pat2[s2, p + NB * a] * pat1[parent, p + NB * a]).astype(F32)
        ew[:, pl.ds(B * a, B)] = (l2_ref[pl.ds(B * a, B), :] * ma).T

    @pl.loop(0, NB)
    def _(k):
        right = right3(jnp.concatenate([g1[0, k], g1[1, k]], axis=1))
        ew[...] -= dot(left3(bz[k]), right)

    ge[0, q] = ew[:, :B]
    ge[1, q] = ew[:, B:]

    def second_level():
        yield from gather(ge, M_GE)
        times_root(ge, p2)
        yield from reduce(p2, x2, rp2, rm2, M_Y2)
        transpose_out(p2, yt2, M_T2)
        yield

    def first_level():
        times_root(g1, p1)
        yield from reduce(p1, x1, rp1, rm1, M_Y1)
        transpose_out(p1, yt1, M_T1)
        yield
        right = transpose_in(yt1, M_T1)

        rhs = right

        @pl.loop(0, NB // GROUP)
        def _(i):
            store_halves(pz1, i, dot(left3(panel(g1, i)), rhs))

        yield from reduce(pz1, xz1, rpz1, rmz1, M_Z1)

    def corner():
        for _ in range(6):
            yield
        yield from gather(gbd, M_BD)

    rounds(second_level(), first_level(), corner())

    def corner_step(k, acc):
        return acc + dot(left3(bz[k]), right3(gbd[1, k]))

    u3 = right3(lax.fori_loop(0, NB, corner_step, jnp.zeros((B, B), F32)).T)
    y3 = transpose_in(yt2, M_T2)

    @pl.loop(0, NB // GROUP)
    def _(i):
        rows = pl.ds(i * GROUP, GROUP)
        out = dot(left3(panel(ge, i)), y3)
        out = out + dot(left3(gbd[0, rows].reshape(GROUP * B, B)), u3)
        store_halves(pz2, i, out)

    rounds(reduce(pz2, xz2, rpz2, rmz2, M_Z2))

    finish(pz1, w1, M_F1)
    finish(pz2, w2, M_F2)
    same1 = (seg1[p] == seg1[q]).astype(F32)
    same2 = (seg2[p] == seg2[q]).astype(F32)
    o1_ref[...] = (d1_ref[...] + w1[...].reshape(B, B)) * same1
    o2_ref[...] = (d2_ref[...] + w2[...].reshape(B, B)) * same2

    for copy in pending:
        copy.wait_send()
    transpose_sent(p1, yt1, M_T1)
    transpose_sent(p2, yt2, M_T2)


def on_device(
    root_inverse, lower_one, lower_two, dinv_one, dinv_two,
    seg_one, seg_two, parent_two, pattern_one, pattern_two,
):
    vmem = pl.BlockSpec(memory_space=pltpu.VMEM)
    smem = pl.BlockSpec(memory_space=pltpu.SMEM)

    def buf(*shape, dtype=F32):
        return pltpu.VMEM(shape, dtype)

    def sums(rows):
        return [
            buf(2, NB, rows, B),
            buf(NB, rows, B),
            buf(4, 2, rows, B),
            buf(3, 2, rows, B),
        ]

    outs = pl.pallas_call(
        kernel,
        out_shape=[jax.ShapeDtypeStruct((B, B), F32)] * 2,
        in_specs=[smem] * 5 + [vmem] * 5,
        out_specs=[vmem] * 2,
        scratch_shapes=[
            buf(2, NB, B, B),
            buf(2, NB, B, B),
            buf(2, NB, B, B),
            buf(NB, B, B),
            *sums(B),
            *sums(B),
            *sums(B // 2),
            *sums(B // 2),
            buf(2, B, B),
            buf(2, B, B),
            buf(2, B // 2, B),
            buf(2, B // 2, B),
            buf(6 * B, 2 * B, dtype=BF16),
            buf(B, 2 * B),
            pltpu.SemaphoreType.DMA((M_ALL,)),
            pltpu.SemaphoreType.DMA((M_ALL,)),
        ],
        compiler_params=pltpu.CompilerParams(
            collective_id=0, has_side_effects=True, vmem_limit_bytes=48 << 20
        ),
    )(
        seg_one, seg_two, parent_two, pattern_one, pattern_two,
        root_inverse.reshape(4 * B, B),
        lower_one.reshape(2 * B, B),
        lower_two.reshape(3 * B, B),
        dinv_one.reshape(B, B),
        dinv_two.reshape(B, B),
    )
    return tuple(out.reshape(1, 1, B, 1, 1, B) for out in outs)


def solution(mesh):
    blocks = P(None, "prow", None, None, "pcol", None)
    return jax.shard_map(
        on_device,
        mesh=mesh,
        in_specs=(blocks,) * 5 + (P(),) * 5,
        out_specs=(blocks,) * 2,
        check_vma=False,
    )
```

```python
import jax
import jax.numpy as jnp
from jax import lax
from jax.experimental import pallas as pl
from jax.experimental.pallas import tpu as pltpu
from jax.sharding import PartitionSpec as P

MESH = pl.DeviceIdType.MESH
F32 = jnp.float32
BF16 = jnp.bfloat16
B = 128
NX = 4
NY = 4
NZ = 8
NB = 16

M_ROOT = 0
M_G1 = M_ROOT + 3
M_GE = M_G1 + 30
M_BD = M_GE + 30
M_BZ = M_BD + 30
M_Y1 = M_BZ + 15
M_Y2 = M_Y1 + 20
M_Z1 = M_Y2 + 20
M_Z2 = M_Z1 + 22
M_T1 = M_Z2 + 22
M_T2 = M_T1 + 4
M_F1 = M_T2 + 4
M_F2 = M_F1 + 1
M_ALL = M_F2 + 1
STEPS = (1, 3, 2)
OFFSETS = (0, 3, 1, 2)


def split(x):
    hi = x.astype(BF16)
    lo = (x - hi.astype(F32)).astype(BF16)
    return hi, lo


def left3(x):
    hi, lo = split(x)
    return jnp.concatenate([hi, hi, lo], axis=1)


def right3(x):
    hi, lo = split(x)
    return jnp.concatenate([hi, lo, hi], axis=0)


def dot(a, b):
    return jnp.dot(a, b, preferred_element_type=F32)


def until(flow, *others):
    others = list(others)
    for _ in flow:
        for other in list(others):
            if next(other, "end") == "end":
                others.remove(other)


def rounds(*flows):
    flows = list(flows)
    while flows:
        for flow in list(flows):
            try:
                next(flow)
            except StopIteration:
                flows.remove(flow)


def kernel(
    seg1, seg2, par2, pat1, pat2,
    r_hbm, l1_hbm, l2_hbm, d1_hbm, d2_hbm,
    o1_ref, o2_ref,
    r_ref, l1_ref, l2_ref, d1_ref, d2_ref,
    gr, g1, ge, gbd, bz,
    p1, x1, ch1,
    p2, x2, ch2,
    pz1, xz1, upz1, dnz1,
    pz2, xz2, upz2, dnz2,
    yt1, yt2, w1, w2, ew,
    send, recv, local,
):
    p = lax.axis_index("prow")
    q = lax.axis_index("pcol")
    z = p // 2
    c = p % 2
    y = q // NX
    x = q % NX
    lands = (z + x // 2) % 2 == 0
    odd = jnp.where(lands, 0, 1)
    sibling = (2 * z + 1 - c, q)
    z_up = (2 * ((z + 1) % NZ) + c, q)
    z_down = (2 * ((z + NZ - 1) % NZ) + c, q)
    pending = []
    drains = []

    def at(dx, dy):
        return (p, ((y + dy) % NY) * NX + (x + dx) % NX)

    barrier = pltpu.get_barrier_semaphore()
    partners = [at(1, 0), at(2, 0), at(3, 0), at(0, 1), at(0, 2), at(0, 3)]
    partners += [sibling, z_up, z_down]
    partners += [(2 * z + 1 - c, y * NX + (x + d) % NX) for d in (1, 2, 3)]
    for device in partners:
        pl.semaphore_signal(barrier, inc=1, device_id=device, device_id_type=MESH)

    loads = [
        pltpu.make_async_copy(src, dst, local.at[n])
        for n, (src, dst) in enumerate(
            [(r_hbm, r_ref), (l1_hbm, l1_ref), (l2_hbm, l2_ref), (d1_hbm, d1_ref), (d2_hbm, d2_ref)]
        )
    ]
    for copy in loads:
        copy.start()

    def remote(m, src, dst, device, arrival=None):
        return pltpu.make_async_remote_copy(
            src_ref=src,
            dst_ref=dst,
            send_sem=send.at[m],
            recv_sem=recv.at[m if arrival is None else arrival],
            device_id=device,
            device_id_type=MESH,
        )

    def push(m, src, dst, device, arrival=None):
        copy = remote(m, src, dst, device, arrival)
        copy.start()
        pending.append(copy)

    def arrive(m, dst):
        remote(m, dst, dst, sibling).wait_recv()

    s1 = seg1[q]
    s2 = seg2[q]
    parent = par2[s2]
    loads[1].wait()
    for a in range(2):
        m1 = pat1[s1, p + NB * a].astype(F32)
        g1[q, a] = (l1_ref[pl.ds(B * a, B), :] * m1).T
    mb = (pat2[s2, 2 * NB + p] * (seg1[p] == parent).astype(jnp.int32)).astype(F32)
    loads[2].wait()
    own_b = (l2_ref[pl.ds(2 * B, B), :] * mb).T
    bz[p] = own_b
    pl.semaphore_wait(barrier, len(partners))

    def prepare_root():
        loads[0].wait()
        for a in range(2):
            gr[y, a] = r_ref[pl.ds(a, 2 * B, stride=2), :].T

    def prepare_rest():
        gbd[q, 0] = own_b
        for a in range(2):
            ma = (pat2[s2, p + NB * a] * pat1[parent, p + NB * a]).astype(F32)
            ew[:, pl.ds(B * a, B)] = (l2_ref[pl.ds(B * a, B), :] * ma).T
        loads[3].wait()
        gbd[q, 1] = d1_ref[...].T
        loads[4].wait()

    def gather_root():
        for n, step in enumerate(STEPS):
            push(M_ROOT + n, gr.at[y], gr.at[y], at(0, step))
        yield
        for n, step in enumerate(STEPS):
            arrive(M_ROOT + n, gr.at[(y + NY - step) % NY])

    def gather(g, base):
        def slot(h, du, dv):
            dx, dy = (du, dv) if h == 0 else (dv, du)
            return g.at[((y + dy) % NY) * NX + (x + dx) % NX, h]

        def first(h, n):
            view = slot(h, 0, 0)
            step = STEPS[n]
            push(base + 15 * h + n, view, view, at(step, 0) if h == 0 else at(0, step))

        def second(h, i, n):
            view = slot(h, OFFSETS[i], 0)
            step = STEPS[n]
            push(base + 15 * h + 3 + 3 * i + n, view, view, at(0, step) if h == 0 else at(step, 0))

        def got_first(h, n):
            arrive(base + 15 * h + n, slot(h, 4 - STEPS[n], 0))

        def got_second(h, i, n):
            arrive(base + 15 * h + 3 + 3 * i + n, slot(h, OFFSETS[i], 4 - STEPS[n]))

        for n in range(3):
            first(0, n)
            second(1, 0, n)
        for n in range(3):
            first(1, n)
            second(0, 0, n)
        yield
        for n in range(3):
            for h in range(2):
                got_first(h, n)
                for m in range(3):
                    second(h, 1 + n, m)
        for n in range(3):
            got_second(1, 0, n)
        yield
        for n in range(3):
            got_second(0, 0, n)
        for i in range(1, 4):
            for n in range(3):
                for h in range(2):
                    got_second(h, i, n)

    def column():
        def slot(dz, core):
            return bz.at[2 * ((z + dz + NZ) % NZ) + core]

        def send_to(m, dz, device):
            view = slot(dz, c)
            push(M_BZ + m, view, view, device)

        send_to(0, 0, z_up)
        send_to(4, 0, z_down)
        send_to(7, 0, sibling)
        yield
        for t in range(1, 5):
            arrive(M_BZ + t - 1, slot(-t, c))
            if t < 4:
                send_to(t, -t, z_up)
            send_to(7 + t, -t, sibling)
            if t < 4:
                arrive(M_BZ + 4 + t - 1, slot(t, c))
                if t < 3:
                    send_to(4 + t, t, z_down)
                send_to(11 + t, t, sibling)
            yield
        arrive(M_BZ + 7, slot(0, 1 - c))
        for t in range(1, 5):
            arrive(M_BZ + 7 + t, slot(-t, 1 - c))
            if t < 4:
                arrive(M_BZ + 11 + t, slot(t, 1 - c))

    def reduce(part, other, up, down, base):
        order = (4, -3, 3, -2, 2, -1, 1, 0)

        def there(off):
            return (z + off + NZ) % NZ

        for n, off in enumerate(order):
            push(base + n, part.at[1 - c, there(off)], other.at[there(off)], sibling)
        yield

        def own(n, i):
            d = there(order[n])
            if i == 0:
                arrive(base + n, other.at[d])
            return part[c, d, i] + other[d, i]

        def hop(n, t, i, buffer, m, device):
            total = own(n, i)
            if t > 0:
                arrive(m + 2 * (t - 1) + i, buffer.at[t - 1, i])
                total = total + buffer[t - 1, i]
            d = there(order[n])
            part[c, d, i] = total
            push(m + 2 * t + i, part.at[c, d, i], buffer.at[t, i], device)

        for t in range(4):
            for i in range(2):
                hop(2 * t, t, i, up, base + 8, z_up)
                if t < 3:
                    hop(2 * t + 1, t, i, down, base + 16, z_down)
            yield
        for i in range(2):
            total = own(7, i)
            arrive(base + 20 + i, down.at[2, i])
            total = total + down[2, i]
            arrive(base + 14 + i, up.at[3, i])
            part[c, z, i] = total + up[3, i]

    def reduce_panel(part, other, chain, base):
        UP, DOWN = 0, 2
        offsets = (4 - odd, 2 - 5 * odd, 3 * odd - 2, 0 - odd)
        rows = [((z + off + NZ) % NZ) // 2 for off in offsets]
        even_sent, odd_sent = [], []
        odd_chip = jnp.logical_not(lands)

        def wait_own(n):
            arrive(base + n, other.at[rows[n]])

        def own(n, i):
            return part[c, rows[n], i] + other[rows[n], i]

        def got(kind, i):
            arrive(base + 4 + 4 * kind + i, chain.at[kind, i])
            return chain[kind, i]

        def onward(sent, n, i, kind, total):
            part[c, rows[n], i] = total
            device = z_up if kind < DOWN else z_down
            copy = remote(
                base + 4 + 4 * kind + i, part.at[c, rows[n], i], chain.at[kind, i], device
            )
            copy.start()
            sent.append((base + 4 + 4 * kind + i, rows[n], i, kind))

        for n in range(4):
            push(base + n, part.at[1 - c, rows[n]], other.at[rows[n]], sibling)
        yield

        @pl.when(lands)
        def _():
            wait_own(0)
            for i in range(2):
                onward(even_sent, 0, i, UP, own(0, i))
                onward(even_sent, 0, i + 2, DOWN, own(0, i + 2))

        @pl.when(odd_chip)
        def _():
            wait_own(0)
            wait_own(1)
            for i in range(2):
                onward(odd_sent, 0, i + 2, UP, own(0, i + 2))
                onward(odd_sent, 1, i, DOWN, own(1, i))

        yield

        @pl.when(odd_chip)
        def _():
            for i in range(2):
                onward(odd_sent, 0, i, UP, own(0, i) + got(UP, i))
                onward(odd_sent, 1, i + 2, DOWN, own(1, i + 2) + got(DOWN, i + 2))

        @pl.when(lands)
        def _():
            wait_own(1)
            wait_own(2)
            for i in range(2):
                onward(even_sent, 1, i + 2, UP + 1, own(1, i + 2) + got(UP, i + 2))
                onward(even_sent, 2, i, DOWN + 1, own(2, i) + got(DOWN, i))

        yield

        @pl.when(odd_chip)
        def _():
            wait_own(2)
            wait_own(3)
            for i in range(2):
                onward(odd_sent, 2, i + 2, UP + 1, own(2, i + 2) + got(UP + 1, i + 2))
                onward(odd_sent, 3, i, DOWN + 1, own(3, i) + got(DOWN + 1, i))

        @pl.when(lands)
        def _():
            for i in range(2):
                onward(even_sent, 1, i, UP + 1, own(1, i) + got(UP, i))
                onward(even_sent, 2, i + 2, DOWN + 1, own(2, i + 2) + got(DOWN, i + 2))

        yield

        @pl.when(odd_chip)
        def _():
            for i in range(2):
                onward(odd_sent, 2, i, UP + 1, own(2, i) + got(UP + 1, i))
                onward(odd_sent, 3, i + 2, DOWN + 1, own(3, i + 2) + got(DOWN + 1, i + 2))

        yield

        @pl.when(lands)
        def _():
            wait_own(3)
            for i in range(4):
                part[c, rows[3], i] = own(3, i) + got(UP + 1, i) + got(DOWN + 1, i)

        def drain():
            for condition, sent in ((lands, even_sent), (odd_chip, odd_sent)):
                @pl.when(condition)
                def _():
                    for m, row, i, kind in sent:
                        remote(m, part.at[c, row, i], chain.at[kind, i], z_up).wait_send()

        drains.append(drain)

    core = x % 2
    keeps = lands & (c == core)

    def hand_over(part, yt, base):
        for step in (1, 3, 2):
            @pl.when(lands)
            def _():
                i = (x + step) % NX
                remote(
                    base + step, part.at[c, z // 2, i], yt.at[c], (2 * z + core, y * NX + i), base + c
                ).start()

        @pl.when(keeps)
        def _():
            yt[c] = part[c, z // 2, x]

        @pl.when(lands & (c != core))
        def _():
            remote(base, part.at[c, z // 2, x], yt.at[c], sibling, base + c).start()

    def handed_over(part, yt, base):
        @pl.when(lands)
        def _():
            for step in (1, 3, 2):
                i = (x + step) % NX
                remote(
                    base + step, part.at[c, z // 2, i], yt.at[c], (2 * z + core, y * NX + i), base + c
                ).wait_send()

        @pl.when(lands & (c != core))
        def _():
            remote(base, part.at[c, z // 2, x], yt.at[c], sibling, base + c).wait_send()

    def take(yt, base):
        arrive(base + 1 - c, yt.at[1 - c])

        @pl.when(jnp.logical_not(keeps))
        def _():
            arrive(base + c, yt.at[c])

        return right3(yt[...].reshape(2 * B, B))

    GROUP = 4

    def panel(g, i):
        rows = pl.ds(i * GROUP, GROUP)
        return jnp.concatenate(
            [g[rows, 0].reshape(GROUP * B, B), g[rows, 1].reshape(GROUP * B, B)], axis=1
        )

    def times_root(g, part):
        right = right3(
            jnp.concatenate(
                [
                    jnp.concatenate([g[y * NX + i, 0].T, g[y * NX + i, 1].T], axis=0)
                    for i in range(NX)
                ],
                axis=1,
            )
        )
        for a in range(2):
            out = dot(left3(gr[:, a].reshape(NY * B, 2 * B)), right)
            for i in range(NX):
                part[a, :, i] = out[:, B * i : B * i + B].reshape(NY, B, B)

    def store_halves(part, i, out):
        rows = pl.ds(i * 2, 2)
        blocks = out.reshape(2, 2, B, B)
        part[0, rows] = blocks[:, :, : B // 2]
        part[1, rows] = blocks[:, :, B // 2 :]

    def finish(part, w, base):
        push(base, part.at[c, z, 1 - c], w.at[c], sibling)
        w[c] = part[c, z, c]
        arrive(base, w.at[1 - c])

    first, bcol, root = gather(g1, M_G1), column(), gather_root()
    whole, bd = gather(ge, M_GE), gather(gbd, M_BD)
    next(first)
    next(bcol)
    prepare_root()
    prepare_rest()
    next(first)
    next(root)
    rounds(bcol, first)
    next(bd)

    @pl.loop(0, NB)
    def _(k):
        right = right3(jnp.concatenate([g1[k, 0], g1[k, 1]], axis=1))
        ew[...] -= dot(left3(bz[k]), right)

    ge[q, 0] = ew[:, :B]
    ge[q, 1] = ew[:, B:]
    next(whole)
    rounds(root)
    times_root(g1, p1)

    def first_level():
        yield from reduce_panel(p1, x1, ch1, M_Y1)
        hand_over(p1, yt1, M_T1)
        yield
        right = take(yt1, M_T1)

        @pl.loop(0, NB // GROUP)
        def _(i):
            store_halves(pz1, i, dot(left3(panel(g1, i)), right))

        yield from reduce(pz1, xz1, upz1, dnz1, M_Z1)

    def second_level():
        yield from reduce_panel(p2, x2, ch2, M_Y2)
        hand_over(p2, yt2, M_T2)

    level_one, level_two = first_level(), second_level()
    next(level_one)
    next(level_one)
    next(whole)
    next(bd)
    times_root(ge, p2)
    next(level_two)
    until(level_two, level_one)
    rounds(bd, whole)

    def corner_step(k, acc):
        return acc + dot(left3(bz[k]), right3(gbd[k, 1]))

    u3 = right3(lax.fori_loop(0, NB, corner_step, jnp.zeros((B, B), F32)).T)
    y3 = take(yt2, M_T2)

    @pl.loop(0, NB // GROUP)
    def _(i):
        out = dot(left3(panel(ge, i)), y3)
        out = out + dot(left3(gbd[pl.ds(i * GROUP, GROUP), 0].reshape(GROUP * B, B)), u3)
        store_halves(pz2, i, out)

    rounds(reduce(pz2, xz2, upz2, dnz2, M_Z2), level_one)

    finish(pz1, w1, M_F1)
    finish(pz2, w2, M_F2)
    same1 = (seg1[p] == seg1[q]).astype(F32)
    same2 = (seg2[p] == seg2[q]).astype(F32)
    o1_ref[...] = (d1_ref[...] + w1[...].reshape(B, B)) * same1
    o2_ref[...] = (d2_ref[...] + w2[...].reshape(B, B)) * same2

    for copy in pending:
        copy.wait_send()
    for drain in drains:
        drain()
    handed_over(p1, yt1, M_T1)
    handed_over(p2, yt2, M_T2)


def on_device(
    root_inverse, lower_one, lower_two, dinv_one, dinv_two,
    seg_one, seg_two, parent_two, pattern_one, pattern_two,
):
    vmem = pl.BlockSpec(memory_space=pltpu.VMEM)
    smem = pl.BlockSpec(memory_space=pltpu.SMEM)
    hbm = pl.BlockSpec(memory_space=pltpu.HBM)

    def buf(*shape):
        return pltpu.VMEM(shape, F32)

    panel_sum = [buf(2, NY, NX, B, B), buf(NY, NX, B, B), buf(4, NX, B, B)]
    half = B // 2
    block_sum = [
        buf(2, NZ, 2, half, B),
        buf(NZ, 2, half, B),
        buf(4, 2, half, B),
        buf(3, 2, half, B),
    ]

    outs = pl.pallas_call(
        kernel,
        out_shape=[jax.ShapeDtypeStruct((B, B), F32)] * 2,
        in_specs=[smem] * 5 + [hbm] * 5,
        out_specs=[vmem] * 2,
        scratch_shapes=[
            buf(4 * B, B),
            buf(2 * B, B),
            buf(3 * B, B),
            buf(B, B),
            buf(B, B),
            buf(NY, 2, B, 2 * B),
            buf(NB, 2, B, B),
            buf(NB, 2, B, B),
            buf(NB, 2, B, B),
            buf(NB, B, B),
            *panel_sum,
            *panel_sum,
            *block_sum,
            *block_sum,
            buf(2, B, B),
            buf(2, B, B),
            buf(2, B // 2, B),
            buf(2, B // 2, B),
            buf(B, 2 * B),
            pltpu.SemaphoreType.DMA((M_ALL,)),
            pltpu.SemaphoreType.DMA((M_ALL,)),
            pltpu.SemaphoreType.DMA((5,)),
        ],
        compiler_params=pltpu.CompilerParams(
            collective_id=0, has_side_effects=True, vmem_limit_bytes=56 << 20
        ),
    )(
        seg_one, seg_two, parent_two, pattern_one, pattern_two,
        root_inverse.reshape(4 * B, B),
        lower_one.reshape(2 * B, B),
        lower_two.reshape(3 * B, B),
        dinv_one.reshape(B, B),
        dinv_two.reshape(B, B),
    )
    return tuple(out.reshape(1, 1, B, 1, 1, B) for out in outs)


def solution(mesh):
    blocks = P(None, "prow", None, None, "pcol", None)
    return jax.shard_map(
        on_device,
        mesh=mesh,
        in_specs=(blocks,) * 5 + (P(),) * 5,
        out_specs=(blocks,) * 2,
        check_vma=False,
    )
```

```python
import jax
import jax.numpy as jnp
from jax import lax
from jax.experimental import pallas as pl
from jax.experimental.pallas import tpu as pltpu
from jax.sharding import PartitionSpec as P

MESH = pl.DeviceIdType.MESH
F32 = jnp.float32
BF16 = jnp.bfloat16
B = 128
NX = 4
NY = 4
NZ = 8
NB = 16

M_ROOT = 0
M_G1 = M_ROOT + 3
M_GE = M_G1 + 30
M_BD = M_GE + 30
M_BZ = M_BD + 30
M_Y1 = M_BZ + 15
M_Y2 = M_Y1 + 20
M_Z1 = M_Y2 + 20
M_Z2 = M_Z1 + 22
M_T1 = M_Z2 + 22
M_T2 = M_T1 + 4
M_F1 = M_T2 + 4
M_F2 = M_F1 + 1
M_ALL = M_F2 + 1
STEPS = (1, 3, 2)
OFFSETS = (0, 3, 1, 2)


def split(x):
    hi = x.astype(BF16)
    lo = (x - hi.astype(F32)).astype(BF16)
    return hi, lo


def left3(x):
    hi, lo = split(x)
    return jnp.concatenate([hi, hi, lo], axis=1)


def right3(x):
    hi, lo = split(x)
    return jnp.concatenate([hi, lo, hi], axis=0)


def dot(a, b):
    return jnp.dot(a, b, preferred_element_type=F32)


def rounds(*flows):
    flows = list(flows)
    while flows:
        for flow in list(flows):
            try:
                next(flow)
            except StopIteration:
                flows.remove(flow)


def kernel(
    seg1, seg2, par2, pat1, pat2,
    r_hbm, l1_hbm, l2_hbm, d1_hbm, d2_hbm,
    o1_ref, o2_ref,
    r_ref, l1_ref, l2_ref, d1_ref, d2_ref,
    gr, g1, ge, gbd, bz,
    p1, x1, ch1,
    p2, x2, ch2,
    pz1, xz1, upz1, dnz1,
    pz2, xz2, upz2, dnz2,
    yt1, yt2, w1, w2, ew,
    send, recv, local,
):
    p = lax.axis_index("prow")
    q = lax.axis_index("pcol")
    z = p // 2
    c = p % 2
    y = q // NX
    x = q % NX
    lands = (z + x // 2) % 2 == 0
    odd = jnp.where(lands, 0, 1)
    sibling = (2 * z + 1 - c, q)
    z_up = (2 * ((z + 1) % NZ) + c, q)
    z_down = (2 * ((z + NZ - 1) % NZ) + c, q)
    pending = []
    drains = []

    def at(dx, dy):
        return (p, ((y + dy) % NY) * NX + (x + dx) % NX)

    barrier = pltpu.get_barrier_semaphore()
    partners = [at(1, 0), at(2, 0), at(3, 0), at(0, 1), at(0, 2), at(0, 3)]
    partners += [sibling] + [(2 * ((z + d) % NZ) + c, q) for d in range(1, NZ)]
    partners += [(2 * z + 1 - c, y * NX + (x + d) % NX) for d in (1, 2, 3)]
    for device in partners:
        pl.semaphore_signal(barrier, inc=1, device_id=device, device_id_type=MESH)

    loads = [
        pltpu.make_async_copy(src, dst, local.at[n])
        for n, (src, dst) in enumerate(
            [(r_hbm, r_ref), (l1_hbm, l1_ref), (l2_hbm, l2_ref), (d1_hbm, d1_ref), (d2_hbm, d2_ref)]
        )
    ]
    for copy in loads:
        copy.start()

    def remote(m, src, dst, device, arrival=None):
        return pltpu.make_async_remote_copy(
            src_ref=src,
            dst_ref=dst,
            send_sem=send.at[m],
            recv_sem=recv.at[m if arrival is None else arrival],
            device_id=device,
            device_id_type=MESH,
        )

    def push(m, src, dst, device, arrival=None):
        copy = remote(m, src, dst, device, arrival)
        copy.start()
        pending.append(copy)

    def arrive(m, dst):
        remote(m, dst, dst, sibling).wait_recv()

    s1 = seg1[q]
    s2 = seg2[q]
    parent = par2[s2]
    loads[1].wait()
    for a in range(2):
        m1 = pat1[s1, p + NB * a].astype(F32)
        g1[q, pl.ds(B * a, B)] = (l1_ref[pl.ds(B * a, B), :] * m1).T
    mb = (pat2[s2, 2 * NB + p] * (seg1[p] == parent).astype(jnp.int32)).astype(F32)
    loads[2].wait()
    own_b = (l2_ref[pl.ds(2 * B, B), :] * mb).T
    bz[p] = own_b
    pl.semaphore_wait(barrier, len(partners))

    def prepare_root():
        loads[0].wait()
        for a in range(2):
            gr[y, a] = r_ref[pl.ds(a, 2 * B, stride=2), :].T

    def prepare_rest():
        gbd[q, :B] = own_b
        for a in range(2):
            ma = (pat2[s2, p + NB * a] * pat1[parent, p + NB * a]).astype(F32)
            ew[:, pl.ds(B * a, B)] = (l2_ref[pl.ds(B * a, B), :] * ma).T
        loads[3].wait()
        gbd[q, B:] = d1_ref[...].T
        loads[4].wait()

    def gather_root():
        for n, step in enumerate(STEPS):
            push(M_ROOT + n, gr.at[y], gr.at[y], at(0, step))
        yield
        for n, step in enumerate(STEPS):
            arrive(M_ROOT + n, gr.at[(y + NY - step) % NY])

    def gather(g, base, cut=B):
        def slot(h, du, dv):
            dx, dy = (du, dv) if h == 0 else (dv, du)
            rows = pl.ds(0, cut) if h == 0 else pl.ds(cut, 2 * B - cut)
            return g.at[((y + dy) % NY) * NX + (x + dx) % NX, rows]

        def first(h, n):
            view = slot(h, 0, 0)
            step = STEPS[n]
            push(base + 15 * h + n, view, view, at(step, 0) if h == 0 else at(0, step))

        def second(h, i, n):
            view = slot(h, OFFSETS[i], 0)
            step = STEPS[n]
            push(base + 15 * h + 3 + 3 * i + n, view, view, at(0, step) if h == 0 else at(step, 0))

        def got_first(h, n):
            arrive(base + 15 * h + n, slot(h, 4 - STEPS[n], 0))

        def got_second(h, i, n):
            arrive(base + 15 * h + 3 + 3 * i + n, slot(h, OFFSETS[i], 4 - STEPS[n]))

        for n in range(3):
            first(0, n)
            second(1, 0, n)
        for n in range(3):
            first(1, n)
            second(0, 0, n)
        yield
        for n in range(3):
            for h in range(2):
                got_first(h, n)
                for m in range(3):
                    second(h, 1 + n, m)
        for n in range(3):
            got_second(1, 0, n)
        yield
        for n in range(3):
            got_second(0, 0, n)
        for i in range(1, 4):
            for n in range(3):
                for h in range(2):
                    got_second(h, i, n)

    def column():
        turns = (1, 7, 2, 6, 3, 5, 4)

        def slot(turn, core):
            return bz.at[2 * ((z + turn) % NZ) + core]

        for n, turn in enumerate(turns):
            device = (2 * ((z + turn) % NZ) + c, q)
            push(M_BZ + n, slot(0, c), slot(0, c), device)
        push(M_BZ + 7, slot(0, c), slot(0, c), sibling)
        yield
        for n, turn in enumerate(turns):
            arrive(M_BZ + n, slot(NZ - turn, c))
            push(M_BZ + 8 + n, slot(NZ - turn, c), slot(NZ - turn, c), sibling)
        yield
        arrive(M_BZ + 7, slot(0, 1 - c))
        for n, turn in enumerate(turns):
            arrive(M_BZ + 8 + n, slot(NZ - turn, 1 - c))

    def reduce(part, other, up, down, base):
        order = (4, -3, 3, -2, 2, -1, 1, 0)

        def there(off):
            return (z + off + NZ) % NZ

        for n, off in enumerate(order):
            push(base + n, part.at[1 - c, there(off)], other.at[there(off)], sibling)
        yield

        def own(n, i):
            d = there(order[n])
            if i == 0:
                arrive(base + n, other.at[d])
            return part[c, d, i] + other[d, i]

        def hop(n, t, i, buffer, m, device):
            total = own(n, i)
            if t > 0:
                arrive(m + 2 * (t - 1) + i, buffer.at[t - 1, i])
                total = total + buffer[t - 1, i]
            d = there(order[n])
            part[c, d, i] = total
            push(m + 2 * t + i, part.at[c, d, i], buffer.at[t, i], device)

        for t in range(4):
            for i in range(2):
                hop(2 * t, t, i, up, base + 8, z_up)
                if t < 3:
                    hop(2 * t + 1, t, i, down, base + 16, z_down)
            yield
        for i in range(2):
            total = own(7, i)
            arrive(base + 20 + i, down.at[2, i])
            total = total + down[2, i]
            arrive(base + 14 + i, up.at[3, i])
            part[c, z, i] = total + up[3, i]

    def reduce_panel(part, other, chain, base):
        UP, DOWN = 0, 2
        offsets = (4 - odd, 2 - 5 * odd, 3 * odd - 2, 0 - odd)
        rows = [((z + off + NZ) % NZ) // 2 for off in offsets]
        even_sent, odd_sent = [], []
        odd_chip = jnp.logical_not(lands)

        def wait_own(n):
            arrive(base + n, other.at[rows[n]])

        def own(n, i):
            return part[c, rows[n], i] + other[rows[n], i]

        def got(kind, i):
            arrive(base + 4 + 4 * kind + i, chain.at[kind, i])
            return chain[kind, i]

        def onward(sent, n, i, kind, total):
            part[c, rows[n], i] = total
            device = z_up if kind < DOWN else z_down
            copy = remote(
                base + 4 + 4 * kind + i, part.at[c, rows[n], i], chain.at[kind, i], device
            )
            copy.start()
            sent.append((base + 4 + 4 * kind + i, rows[n], i, kind))

        for n in range(4):
            push(base + n, part.at[1 - c, rows[n]], other.at[rows[n]], sibling)
        yield

        @pl.when(lands)
        def _():
            wait_own(0)
            for i in range(2):
                onward(even_sent, 0, i, UP, own(0, i))
                onward(even_sent, 0, i + 2, DOWN, own(0, i + 2))

        @pl.when(odd_chip)
        def _():
            wait_own(0)
            wait_own(1)
            for i in range(2):
                onward(odd_sent, 0, i + 2, UP, own(0, i + 2))
                onward(odd_sent, 1, i, DOWN, own(1, i))

        yield

        @pl.when(odd_chip)
        def _():
            for i in range(2):
                onward(odd_sent, 0, i, UP, own(0, i) + got(UP, i))
                onward(odd_sent, 1, i + 2, DOWN, own(1, i + 2) + got(DOWN, i + 2))

        @pl.when(lands)
        def _():
            wait_own(1)
            wait_own(2)
            for i in range(2):
                onward(even_sent, 1, i + 2, UP + 1, own(1, i + 2) + got(UP, i + 2))
                onward(even_sent, 2, i, DOWN + 1, own(2, i) + got(DOWN, i))

        yield

        @pl.when(odd_chip)
        def _():
            wait_own(2)
            wait_own(3)
            for i in range(2):
                onward(odd_sent, 2, i + 2, UP + 1, own(2, i + 2) + got(UP + 1, i + 2))
                onward(odd_sent, 3, i, DOWN + 1, own(3, i) + got(DOWN + 1, i))

        @pl.when(lands)
        def _():
            for i in range(2):
                onward(even_sent, 1, i, UP + 1, own(1, i) + got(UP, i))
                onward(even_sent, 2, i + 2, DOWN + 1, own(2, i + 2) + got(DOWN, i + 2))

        yield

        @pl.when(odd_chip)
        def _():
            for i in range(2):
                onward(odd_sent, 2, i, UP + 1, own(2, i) + got(UP + 1, i))
                onward(odd_sent, 3, i + 2, DOWN + 1, own(3, i + 2) + got(DOWN + 1, i + 2))

        yield

        @pl.when(lands)
        def _():
            wait_own(3)
            for i in range(4):
                part[c, rows[3], i] = own(3, i) + got(UP + 1, i) + got(DOWN + 1, i)

        def drain():
            for condition, sent in ((lands, even_sent), (odd_chip, odd_sent)):
                @pl.when(condition)
                def _():
                    for m, row, i, kind in sent:
                        remote(m, part.at[c, row, i], chain.at[kind, i], z_up).wait_send()

        drains.append(drain)

    core = x % 2
    keeps = lands & (c == core)

    def hand_over(part, yt, base):
        for step in (1, 3, 2):
            @pl.when(lands)
            def _():
                i = (x + step) % NX
                remote(
                    base + step, part.at[c, z // 2, i], yt.at[c], (2 * z + core, y * NX + i), base + c
                ).start()

        @pl.when(keeps)
        def _():
            yt[c] = part[c, z // 2, x]

        @pl.when(lands & (c != core))
        def _():
            remote(base, part.at[c, z // 2, x], yt.at[c], sibling, base + c).start()

    def handed_over(part, yt, base):
        @pl.when(lands)
        def _():
            for step in (1, 3, 2):
                i = (x + step) % NX
                remote(
                    base + step, part.at[c, z // 2, i], yt.at[c], (2 * z + core, y * NX + i), base + c
                ).wait_send()

        @pl.when(lands & (c != core))
        def _():
            remote(base, part.at[c, z // 2, x], yt.at[c], sibling, base + c).wait_send()

    def take(yt, base):
        arrive(base + 1 - c, yt.at[1 - c])

        @pl.when(jnp.logical_not(keeps))
        def _():
            arrive(base + c, yt.at[c])

        return right3(yt[...].reshape(2 * B, B))

    GROUP = 4

    def panel(g, i):
        rows = pl.ds(i * GROUP, GROUP)
        return jnp.concatenate(
            [g[rows, :B].reshape(GROUP * B, B), g[rows, B:].reshape(GROUP * B, B)], axis=1
        )

    def times_root(g, part):
        right = right3(
            jnp.concatenate(
                [
                    jnp.concatenate([g[y * NX + i, :B].T, g[y * NX + i, B:].T], axis=0)
                    for i in range(NX)
                ],
                axis=1,
            )
        )
        for a in range(2):
            out = dot(left3(gr[:, a].reshape(NY * B, 2 * B)), right)
            for i in range(NX):
                part[a, :, i] = out[:, B * i : B * i + B].reshape(NY, B, B)

    def store_halves(part, i, out):
        rows = pl.ds(i * 2, 2)
        blocks = out.reshape(2, 2, B, B)
        part[0, rows] = blocks[:, :, : B // 2]
        part[1, rows] = blocks[:, :, B // 2 :]

    def finish(part, w, base):
        push(base, part.at[c, z, 1 - c], w.at[c], sibling)
        w[c] = part[c, z, c]
        arrive(base, w.at[1 - c])

    first, bcol, root = gather(g1, M_G1, 64), column(), gather_root()
    whole, bd = gather(ge, M_GE), gather(gbd, M_BD)
    next(first)
    next(bcol)
    prepare_root()
    next(first)
    next(root)
    prepare_rest()
    next(bcol)
    rounds(first, bcol)
    next(bd)

    @pl.loop(0, NB // GROUP)
    def _(i):
        left = jnp.concatenate([bz[i * GROUP + k] for k in range(GROUP)], axis=1)
        ew[...] -= dot(left3(left), right3(panel(g1, i)))

    ge[q, :B] = ew[:, :B]
    ge[q, B:] = ew[:, B:]
    next(whole)
    rounds(root)
    times_root(g1, p1)

    def first_level():
        yield from reduce_panel(p1, x1, ch1, M_Y1)
        hand_over(p1, yt1, M_T1)

    def second_level():
        yield from reduce_panel(p2, x2, ch2, M_Y2)
        hand_over(p2, yt2, M_T2)

    level_one, level_two = first_level(), second_level()
    next(level_one)
    next(level_one)
    next(level_one)
    next(whole)
    next(bd)
    times_root(ge, p2)
    next(level_two)
    next(level_two)
    rounds(level_one, level_two)
    rounds(bd, whole)

    def corner_step(k, acc):
        return acc + dot(left3(bz[k]), right3(gbd[k, B:]))

    u3 = right3(lax.fori_loop(0, NB, corner_step, jnp.zeros((B, B), F32)).T)
    y1 = take(yt1, M_T1)

    @pl.loop(0, NB // GROUP)
    def _(i):
        store_halves(pz1, i, dot(left3(panel(g1, i)), y1))

    last_one = reduce(pz1, xz1, upz1, dnz1, M_Z1)
    next(last_one)
    y3 = take(yt2, M_T2)

    @pl.loop(0, NB // GROUP)
    def _(i):
        out = dot(left3(panel(ge, i)), y3)
        out = out + dot(left3(gbd[pl.ds(i * GROUP, GROUP), :B].reshape(GROUP * B, B)), u3)
        store_halves(pz2, i, out)

    rounds(reduce(pz2, xz2, upz2, dnz2, M_Z2), last_one)

    finish(pz1, w1, M_F1)
    finish(pz2, w2, M_F2)
    same1 = (seg1[p] == seg1[q]).astype(F32)
    same2 = (seg2[p] == seg2[q]).astype(F32)
    o1_ref[...] = (d1_ref[...] + w1[...].reshape(B, B)) * same1
    o2_ref[...] = (d2_ref[...] + w2[...].reshape(B, B)) * same2

    for copy in pending:
        copy.wait_send()
    for drain in drains:
        drain()
    handed_over(p1, yt1, M_T1)
    handed_over(p2, yt2, M_T2)


def on_device(
    root_inverse, lower_one, lower_two, dinv_one, dinv_two,
    seg_one, seg_two, parent_two, pattern_one, pattern_two,
):
    vmem = pl.BlockSpec(memory_space=pltpu.VMEM)
    smem = pl.BlockSpec(memory_space=pltpu.SMEM)
    hbm = pl.BlockSpec(memory_space=pltpu.HBM)

    def buf(*shape):
        return pltpu.VMEM(shape, F32)

    panel_sum = [buf(2, NY, NX, B, B), buf(NY, NX, B, B), buf(4, NX, B, B)]
    half = B // 2
    block_sum = [
        buf(2, NZ, 2, half, B),
        buf(NZ, 2, half, B),
        buf(4, 2, half, B),
        buf(3, 2, half, B),
    ]

    outs = pl.pallas_call(
        kernel,
        out_shape=[jax.ShapeDtypeStruct((B, B), F32)] * 2,
        in_specs=[smem] * 5 + [hbm] * 5,
        out_specs=[vmem] * 2,
        scratch_shapes=[
            buf(4 * B, B),
            buf(2 * B, B),
            buf(3 * B, B),
            buf(B, B),
            buf(B, B),
            buf(NY, 2, B, 2 * B),
            buf(NB, 2 * B, B),
            buf(NB, 2 * B, B),
            buf(NB, 2 * B, B),
            buf(NB, B, B),
            *panel_sum,
            *panel_sum,
            *block_sum,
            *block_sum,
            buf(2, B, B),
            buf(2, B, B),
            buf(2, B // 2, B),
            buf(2, B // 2, B),
            buf(B, 2 * B),
            pltpu.SemaphoreType.DMA((M_ALL,)),
            pltpu.SemaphoreType.DMA((M_ALL,)),
            pltpu.SemaphoreType.DMA((5,)),
        ],
        compiler_params=pltpu.CompilerParams(
            collective_id=0, has_side_effects=True, vmem_limit_bytes=56 << 20
        ),
    )(
        seg_one, seg_two, parent_two, pattern_one, pattern_two,
        root_inverse.reshape(4 * B, B),
        lower_one.reshape(2 * B, B),
        lower_two.reshape(3 * B, B),
        dinv_one.reshape(B, B),
        dinv_two.reshape(B, B),
    )
    return tuple(out.reshape(1, 1, B, 1, 1, B) for out in outs)


def solution(mesh):
    blocks = P(None, "prow", None, None, "pcol", None)
    return jax.shard_map(
        on_device,
        mesh=mesh,
        in_specs=(blocks,) * 5 + (P(),) * 5,
        out_specs=(blocks,) * 2,
        check_vma=False,
    )
```

```python
import jax
import jax.numpy as jnp
from jax import lax
from jax.experimental import pallas as pl
from jax.experimental.pallas import tpu as pltpu
from jax.sharding import PartitionSpec as P

MESH = pl.DeviceIdType.MESH
F32 = jnp.float32
BF16 = jnp.bfloat16
B = 128
NX = 4
NY = 4
NZ = 8
NB = 16

M_ROOT = 0
M_G1 = M_ROOT + 3
M_GE = M_G1 + 30
M_BD = M_GE + 30
M_BZ = M_BD + 30
M_Y1 = M_BZ + 15
M_Y2 = M_Y1 + 20
M_Z1 = M_Y2 + 20
M_Z2 = M_Z1 + 22
M_T1 = M_Z2 + 22
M_T2 = M_T1 + 4
M_F1 = M_T2 + 4
M_F2 = M_F1 + 1
M_ALL = M_F2 + 1
STEPS = (1, 3, 2)
OFFSETS = (0, 3, 1, 2)


def split(x):
    hi = x.astype(BF16)
    lo = (x - hi.astype(F32)).astype(BF16)
    return hi, lo


def left3(x):
    hi, lo = split(x)
    return jnp.concatenate([hi, hi, lo], axis=1)


def right3(x):
    hi, lo = split(x)
    return jnp.concatenate([hi, lo, hi], axis=0)


def dot(a, b):
    return jnp.dot(a, b, preferred_element_type=F32)


def rounds(*flows, between=None):
    flows = list(flows)
    while flows:
        for flow in list(flows):
            try:
                next(flow)
            except StopIteration:
                flows.remove(flow)
        if between is not None:
            between()


def kernel(
    seg1, seg2, par2, pat1, pat2,
    r_hbm, l1_hbm, l2_hbm, d1_hbm, d2_hbm,
    o1_ref, o2_ref,
    r_ref, l1_ref, l2_ref, d1_ref, d2_ref,
    gr, g1, ge, gbd, bz,
    p1, x1, ch1,
    p2, x2, ch2,
    pz1, xz1, upz1, dnz1,
    pz2, xz2, upz2, dnz2,
    yt1, yt2, w1, w2, ew,
    send, recv, local,
):
    p = lax.axis_index("prow")
    q = lax.axis_index("pcol")
    z = p // 2
    c = p % 2
    y = q // NX
    x = q % NX
    lands = (z + x // 2) % 2 == 0
    odd = jnp.where(lands, 0, 1)
    sibling = (2 * z + 1 - c, q)
    z_up = (2 * ((z + 1) % NZ) + c, q)
    z_down = (2 * ((z + NZ - 1) % NZ) + c, q)
    pending = []
    drains = []

    def at(dx, dy):
        return (p, ((y + dy) % NY) * NX + (x + dx) % NX)

    barrier = pltpu.get_barrier_semaphore()
    partners = [at(1, 0), at(2, 0), at(3, 0), at(0, 1), at(0, 2), at(0, 3)]
    partners += [sibling] + [(2 * ((z + d) % NZ) + c, q) for d in range(1, NZ)]
    partners += [(2 * z + 1 - c, y * NX + (x + d) % NX) for d in (1, 2, 3)]
    for device in partners:
        pl.semaphore_signal(barrier, inc=1, device_id=device, device_id_type=MESH)

    loads = [
        pltpu.make_async_copy(src, dst, local.at[n])
        for n, (src, dst) in enumerate(
            [(r_hbm, r_ref), (l1_hbm, l1_ref), (l2_hbm, l2_ref), (d1_hbm, d1_ref), (d2_hbm, d2_ref)]
        )
    ]
    for copy in loads:
        copy.start()

    def remote(m, src, dst, device, arrival=None):
        return pltpu.make_async_remote_copy(
            src_ref=src,
            dst_ref=dst,
            send_sem=send.at[m],
            recv_sem=recv.at[m if arrival is None else arrival],
            device_id=device,
            device_id_type=MESH,
        )

    def push(m, src, dst, device, arrival=None):
        copy = remote(m, src, dst, device, arrival)
        copy.start()
        pending.append(copy)

    def settle(count):
        for copy in pending[:count]:
            copy.wait_send()
        del pending[:count]

    def arrive(m, dst):
        remote(m, dst, dst, sibling).wait_recv()

    s1 = seg1[q]
    s2 = seg2[q]
    parent = par2[s2]
    loads[1].wait()
    for a in range(2):
        m1 = pat1[s1, p + NB * a].astype(F32)
        g1[q, pl.ds(B * a, B)] = (l1_ref[pl.ds(B * a, B), :] * m1).T
    mb = (pat2[s2, 2 * NB + p] * (seg1[p] == parent).astype(jnp.int32)).astype(F32)
    loads[2].wait()
    own_b = (l2_ref[pl.ds(2 * B, B), :] * mb).T
    bz[p] = own_b
    pl.semaphore_wait(barrier, len(partners))

    def prepare_root():
        loads[0].wait()
        for a in range(2):
            gr[y, a] = r_ref[pl.ds(a, 2 * B, stride=2), :].T

    def prepare_rest():
        gbd[q, :B] = own_b
        for a in range(2):
            ma = (pat2[s2, p + NB * a] * pat1[parent, p + NB * a]).astype(F32)
            ew[:, pl.ds(B * a, B)] = (l2_ref[pl.ds(B * a, B), :] * ma).T
        loads[3].wait()
        gbd[q, B:] = d1_ref[...].T
        loads[4].wait()

    def gather_root():
        for n, step in enumerate(STEPS):
            push(M_ROOT + n, gr.at[y], gr.at[y], at(0, step))
        yield
        for n, step in enumerate(STEPS):
            arrive(M_ROOT + n, gr.at[(y + NY - step) % NY])

    def gather(g, base, cut=B):
        def slot(h, du, dv):
            dx, dy = (du, dv) if h == 0 else (dv, du)
            rows = pl.ds(0, cut) if h == 0 else pl.ds(cut, 2 * B - cut)
            return g.at[((y + dy) % NY) * NX + (x + dx) % NX, rows]

        def first(h, n):
            view = slot(h, 0, 0)
            step = STEPS[n]
            push(base + 15 * h + n, view, view, at(step, 0) if h == 0 else at(0, step))

        def second(h, i, n):
            view = slot(h, OFFSETS[i], 0)
            step = STEPS[n]
            push(base + 15 * h + 3 + 3 * i + n, view, view, at(0, step) if h == 0 else at(step, 0))

        def got_first(h, n):
            arrive(base + 15 * h + n, slot(h, 4 - STEPS[n], 0))

        def got_second(h, i, n):
            arrive(base + 15 * h + 3 + 3 * i + n, slot(h, OFFSETS[i], 4 - STEPS[n]))

        for n in range(3):
            first(0, n)
            second(1, 0, n)
        for n in range(3):
            first(1, n)
            second(0, 0, n)
        yield
        for n in range(3):
            for h in range(2):
                got_first(h, n)
                for m in range(3):
                    second(h, 1 + n, m)
        for n in range(3):
            got_second(1, 0, n)
        yield
        for n in range(3):
            got_second(0, 0, n)
        for i in range(1, 4):
            for n in range(3):
                for h in range(2):
                    got_second(h, i, n)

    def column():
        turns = (1, 7, 2, 6, 3, 5, 4)

        def slot(turn, core):
            return bz.at[2 * ((z + turn) % NZ) + core]

        for n, turn in enumerate(turns):
            device = (2 * ((z + turn) % NZ) + c, q)
            push(M_BZ + n, slot(0, c), slot(0, c), device)
        push(M_BZ + 7, slot(0, c), slot(0, c), sibling)
        yield
        for n, turn in enumerate(turns):
            arrive(M_BZ + n, slot(NZ - turn, c))
            push(M_BZ + 8 + n, slot(NZ - turn, c), slot(NZ - turn, c), sibling)
        yield
        arrive(M_BZ + 7, slot(0, 1 - c))
        for n, turn in enumerate(turns):
            arrive(M_BZ + 8 + n, slot(NZ - turn, 1 - c))

    def reduce(part, other, up, down, base):
        order = (4, -3, 3, -2, 2, -1, 1, 0)

        def there(off):
            return (z + off + NZ) % NZ

        for n, off in enumerate(order):
            push(base + n, part.at[1 - c, there(off)], other.at[there(off)], sibling)
        yield

        def own(n, i):
            d = there(order[n])
            if i == 0:
                arrive(base + n, other.at[d])
            return part[c, d, i] + other[d, i]

        def hop(n, t, i, buffer, m, device):
            total = own(n, i)
            if t > 0:
                arrive(m + 2 * (t - 1) + i, buffer.at[t - 1, i])
                total = total + buffer[t - 1, i]
            d = there(order[n])
            part[c, d, i] = total
            push(m + 2 * t + i, part.at[c, d, i], buffer.at[t, i], device)

        for t in range(4):
            for i in range(2):
                hop(2 * t, t, i, up, base + 8, z_up)
                if t < 3:
                    hop(2 * t + 1, t, i, down, base + 16, z_down)
            yield
        for i in range(2):
            total = own(7, i)
            arrive(base + 20 + i, down.at[2, i])
            total = total + down[2, i]
            arrive(base + 14 + i, up.at[3, i])
            part[c, z, i] = total + up[3, i]

    def reduce_panel(part, other, chain, base, product):
        UP, DOWN = 0, 2
        offsets = (4 - odd, 2 - 5 * odd, 3 * odd - 2, 0 - odd)
        rows = [((z + off + NZ) % NZ) // 2 for off in offsets]
        even_sent, odd_sent = [], []
        odd_chip = jnp.logical_not(lands)

        def wait_own(n):
            arrive(base + n, other.at[rows[n]])

        def own(n, i):
            return part[c, rows[n], i] + other[rows[n], i]

        def got(kind, i):
            arrive(base + 4 + 4 * kind + i, chain.at[kind, i])
            return chain[kind, i]

        def onward(sent, n, i, kind, total):
            part[c, rows[n], i] = total
            device = z_up if kind < DOWN else z_down
            copy = remote(
                base + 4 + 4 * kind + i, part.at[c, rows[n], i], chain.at[kind, i], device
            )
            copy.start()
            sent.append((base + 4 + 4 * kind + i, rows[n], i, kind))

        product(1 - c)
        for n in range(4):
            push(base + n, part.at[1 - c, rows[n]], other.at[rows[n]], sibling)
        product(c)
        yield

        @pl.when(lands)
        def _():
            wait_own(0)
            for i in range(2):
                onward(even_sent, 0, i, UP, own(0, i))
                onward(even_sent, 0, i + 2, DOWN, own(0, i + 2))

        @pl.when(odd_chip)
        def _():
            wait_own(0)
            wait_own(1)
            for i in range(2):
                onward(odd_sent, 0, i + 2, UP, own(0, i + 2))
                onward(odd_sent, 1, i, DOWN, own(1, i))

        yield

        @pl.when(odd_chip)
        def _():
            for i in range(2):
                onward(odd_sent, 0, i, UP, own(0, i) + got(UP, i))
                onward(odd_sent, 1, i + 2, DOWN, own(1, i + 2) + got(DOWN, i + 2))

        @pl.when(lands)
        def _():
            wait_own(1)
            wait_own(2)
            for i in range(2):
                onward(even_sent, 1, i + 2, UP + 1, own(1, i + 2) + got(UP, i + 2))
                onward(even_sent, 2, i, DOWN + 1, own(2, i) + got(DOWN, i))

        yield

        @pl.when(odd_chip)
        def _():
            wait_own(2)
            wait_own(3)
            for i in range(2):
                onward(odd_sent, 2, i + 2, UP + 1, own(2, i + 2) + got(UP + 1, i + 2))
                onward(odd_sent, 3, i, DOWN + 1, own(3, i) + got(DOWN + 1, i))

        @pl.when(lands)
        def _():
            for i in range(2):
                onward(even_sent, 1, i, UP + 1, own(1, i) + got(UP, i))
                onward(even_sent, 2, i + 2, DOWN + 1, own(2, i + 2) + got(DOWN, i + 2))

        yield

        @pl.when(odd_chip)
        def _():
            for i in range(2):
                onward(odd_sent, 2, i, UP + 1, own(2, i) + got(UP + 1, i))
                onward(odd_sent, 3, i + 2, DOWN + 1, own(3, i + 2) + got(DOWN + 1, i + 2))

        yield

        @pl.when(lands)
        def _():
            wait_own(3)
            for i in range(4):
                part[c, rows[3], i] = own(3, i) + got(UP + 1, i) + got(DOWN + 1, i)

        def drain():
            for condition, sent in ((lands, even_sent), (odd_chip, odd_sent)):
                @pl.when(condition)
                def _():
                    for m, row, i, kind in sent:
                        remote(m, part.at[c, row, i], chain.at[kind, i], z_up).wait_send()

        drains.append(drain)

    core = x % 2
    keeps = lands & (c == core)

    def hand_over(part, yt, base):
        for step in (1, 3, 2):
            @pl.when(lands)
            def _():
                i = (x + step) % NX
                remote(
                    base + step, part.at[c, z // 2, i], yt.at[c], (2 * z + core, y * NX + i), base + c
                ).start()

        @pl.when(keeps)
        def _():
            yt[c] = part[c, z // 2, x]

        @pl.when(lands & (c != core))
        def _():
            remote(base, part.at[c, z // 2, x], yt.at[c], sibling, base + c).start()

    def handed_over(part, yt, base):
        @pl.when(lands)
        def _():
            for step in (1, 3, 2):
                i = (x + step) % NX
                remote(
                    base + step, part.at[c, z // 2, i], yt.at[c], (2 * z + core, y * NX + i), base + c
                ).wait_send()

        @pl.when(lands & (c != core))
        def _():
            remote(base, part.at[c, z // 2, x], yt.at[c], sibling, base + c).wait_send()

    def take(yt, base):
        arrive(base + 1 - c, yt.at[1 - c])

        @pl.when(jnp.logical_not(keeps))
        def _():
            arrive(base + c, yt.at[c])

        return right3(yt[...].reshape(2 * B, B))

    GROUP = 4

    def panel(g, i):
        rows = pl.ds(i * GROUP, GROUP)
        return jnp.concatenate(
            [g[rows, :B].reshape(GROUP * B, B), g[rows, B:].reshape(GROUP * B, B)], axis=1
        )

    def times_root(g, part):
        right = right3(
            jnp.concatenate(
                [
                    jnp.concatenate([g[y * NX + i, :B].T, g[y * NX + i, B:].T], axis=0)
                    for i in range(NX)
                ],
                axis=1,
            )
        )

        def product(a):
            out = dot(left3(gr[:, a].reshape(NY * B, 2 * B)), right)
            for i in range(NX):
                part[a, :, i] = out[:, B * i : B * i + B].reshape(NY, B, B)

        return product

    def store_halves(part, i, out):
        rows = pl.ds(i * 2, 2)
        blocks = out.reshape(2, 2, B, B)
        part[0, rows] = blocks[:, :, : B // 2]
        part[1, rows] = blocks[:, :, B // 2 :]

    def finish(part, w, base):
        push(base, part.at[c, z, 1 - c], w.at[c], sibling)
        w[c] = part[c, z, c]
        arrive(base, w.at[1 - c])

    first, bcol, root = gather(g1, M_G1, 64), column(), gather_root()
    whole, bd = gather(ge, M_GE), gather(gbd, M_BD)
    next(first)
    next(bcol)
    prepare_root()
    next(first)
    next(root)
    prepare_rest()
    next(bcol)
    next(bd)
    rounds(first, bcol)

    @pl.loop(0, NB // GROUP)
    def _(i):
        left = jnp.concatenate([bz[i * GROUP + k] for k in range(GROUP)], axis=1)
        ew[...] -= dot(left3(left), right3(panel(g1, i)))

    ge[q, :B] = ew[:, :B]
    ge[q, B:] = ew[:, B:]
    next(whole)
    rounds(root)

    def first_level():
        yield from reduce_panel(p1, x1, ch1, M_Y1, times_root(g1, p1))
        hand_over(p1, yt1, M_T1)

    def second_level():
        yield from reduce_panel(p2, x2, ch2, M_Y2, times_root(ge, p2))
        hand_over(p2, yt2, M_T2)

    level_one, level_two = first_level(), second_level()
    next(level_one)
    next(level_one)
    next(level_one)
    next(whole)
    next(bd)
    next(level_two)
    next(level_two)
    rounds(level_one, level_two, between=lambda: settle(8))
    rounds(bd, whole)

    def corner_step(k, acc):
        return acc + dot(left3(bz[k]), right3(gbd[k, B:]))

    u3 = right3(lax.fori_loop(0, NB, corner_step, jnp.zeros((B, B), F32)).T)
    y1 = take(yt1, M_T1)

    @pl.loop(0, NB // GROUP)
    def _(i):
        store_halves(pz1, i, dot(left3(panel(g1, i)), y1))

    last_one = reduce(pz1, xz1, upz1, dnz1, M_Z1)
    next(last_one)
    y3 = take(yt2, M_T2)

    @pl.loop(0, NB // GROUP)
    def _(i):
        out = dot(left3(panel(ge, i)), y3)
        out = out + dot(left3(gbd[pl.ds(i * GROUP, GROUP), :B].reshape(GROUP * B, B)), u3)
        store_halves(pz2, i, out)

    rounds(reduce(pz2, xz2, upz2, dnz2, M_Z2), last_one, between=lambda: settle(16))

    finish(pz1, w1, M_F1)
    finish(pz2, w2, M_F2)
    same1 = (seg1[p] == seg1[q]).astype(F32)
    same2 = (seg2[p] == seg2[q]).astype(F32)
    o1_ref[...] = (d1_ref[...] + w1[...].reshape(B, B)) * same1
    o2_ref[...] = (d2_ref[...] + w2[...].reshape(B, B)) * same2

    for copy in pending:
        copy.wait_send()
    for drain in drains:
        drain()
    handed_over(p1, yt1, M_T1)
    handed_over(p2, yt2, M_T2)


def on_device(
    root_inverse, lower_one, lower_two, dinv_one, dinv_two,
    seg_one, seg_two, parent_two, pattern_one, pattern_two,
):
    vmem = pl.BlockSpec(memory_space=pltpu.VMEM)
    smem = pl.BlockSpec(memory_space=pltpu.SMEM)
    hbm = pl.BlockSpec(memory_space=pltpu.HBM)

    def buf(*shape):
        return pltpu.VMEM(shape, F32)

    panel_sum = [buf(2, NY, NX, B, B), buf(NY, NX, B, B), buf(4, NX, B, B)]
    half = B // 2
    block_sum = [
        buf(2, NZ, 2, half, B),
        buf(NZ, 2, half, B),
        buf(4, 2, half, B),
        buf(3, 2, half, B),
    ]

    outs = pl.pallas_call(
        kernel,
        out_shape=[jax.ShapeDtypeStruct((B, B), F32)] * 2,
        in_specs=[smem] * 5 + [hbm] * 5,
        out_specs=[vmem] * 2,
        scratch_shapes=[
            buf(4 * B, B),
            buf(2 * B, B),
            buf(3 * B, B),
            buf(B, B),
            buf(B, B),
            buf(NY, 2, B, 2 * B),
            buf(NB, 2 * B, B),
            buf(NB, 2 * B, B),
            buf(NB, 2 * B, B),
            buf(NB, B, B),
            *panel_sum,
            *panel_sum,
            *block_sum,
            *block_sum,
            buf(2, B, B),
            buf(2, B, B),
            buf(2, B // 2, B),
            buf(2, B // 2, B),
            buf(B, 2 * B),
            pltpu.SemaphoreType.DMA((M_ALL,)),
            pltpu.SemaphoreType.DMA((M_ALL,)),
            pltpu.SemaphoreType.DMA((5,)),
        ],
        compiler_params=pltpu.CompilerParams(
            collective_id=0, has_side_effects=True, vmem_limit_bytes=56 << 20
        ),
    )(
        seg_one, seg_two, parent_two, pattern_one, pattern_two,
        root_inverse.reshape(4 * B, B),
        lower_one.reshape(2 * B, B),
        lower_two.reshape(3 * B, B),
        dinv_one.reshape(B, B),
        dinv_two.reshape(B, B),
    )
    return tuple(out.reshape(1, 1, B, 1, 1, B) for out in outs)


def solution(mesh):
    blocks = P(None, "prow", None, None, "pcol", None)
    return jax.shard_map(
        on_device,
        mesh=mesh,
        in_specs=(blocks,) * 5 + (P(),) * 5,
        out_specs=(blocks,) * 2,
        check_vma=False,
    )
```

```python
import jax
import jax.numpy as jnp
from jax import lax
from jax.experimental import pallas as pl
from jax.experimental.pallas import tpu as pltpu
from jax.sharding import PartitionSpec as P

MESH = pl.DeviceIdType.MESH
F32 = jnp.float32
BF16 = jnp.bfloat16
B = 128
NX = 4
NY = 4
NZ = 8
NB = 16

M_ROOT = 0
M_G1 = M_ROOT + 3
M_GE = M_G1 + 30
M_BD = M_GE + 30
M_BZ = M_BD + 30
M_Y1 = M_BZ + 15
M_Y2 = M_Y1 + 20
M_Z1 = M_Y2 + 20
M_Z2 = M_Z1 + 22
M_T1 = M_Z2 + 22
M_T2 = M_T1 + 4
M_F1 = M_T2 + 4
M_F2 = M_F1 + 1
M_ALL = M_F2 + 1
STEPS = (1, 3, 2)
OFFSETS = (0, 3, 1, 2)


def split(x):
    hi = x.astype(BF16)
    lo = (x - hi.astype(F32)).astype(BF16)
    return hi, lo


def left3(x):
    hi, lo = split(x)
    return jnp.concatenate([hi, hi, lo], axis=1)


def right3(x):
    hi, lo = split(x)
    return jnp.concatenate([hi, lo, hi], axis=0)


def dot(a, b):
    return jnp.dot(a, b, preferred_element_type=F32)


def rounds(*flows):
    flows = list(flows)
    while flows:
        for flow in list(flows):
            try:
                next(flow)
            except StopIteration:
                flows.remove(flow)


def kernel(
    seg1, seg2, par2, pat1, pat2,
    r_hbm, l1_hbm, l2_hbm, d1_hbm, d2_hbm,
    o1_ref, o2_ref,
    r_ref, l1_ref, l2_ref, d1_ref, d2_ref,
    gr, g1, ge, gbd, bz,
    p1, x1, ch1,
    p2, x2, ch2,
    pz1, xz1, upz1, dnz1,
    pz2, xz2, upz2, dnz2,
    yt1, yt2, w1, w2, ew,
    send, recv, local,
):
    p = lax.axis_index("prow")
    q = lax.axis_index("pcol")
    z = p // 2
    c = p % 2
    y = q // NX
    x = q % NX
    lands = (z + x // 2) % 2 == 0
    odd = jnp.where(lands, 0, 1)
    sibling = (2 * z + 1 - c, q)
    z_up = (2 * ((z + 1) % NZ) + c, q)
    z_down = (2 * ((z + NZ - 1) % NZ) + c, q)
    pending = []
    drains = []

    def at(dx, dy):
        return (p, ((y + dy) % NY) * NX + (x + dx) % NX)

    barrier = pltpu.get_barrier_semaphore()
    partners = [at(1, 0), at(2, 0), at(3, 0), at(0, 1), at(0, 2), at(0, 3)]
    partners += [sibling] + [(2 * ((z + d) % NZ) + c, q) for d in range(1, NZ)]
    partners += [(2 * z + 1 - c, y * NX + (x + d) % NX) for d in (1, 2, 3)]
    for device in partners:
        pl.semaphore_signal(barrier, inc=1, device_id=device, device_id_type=MESH)

    loads = [
        pltpu.make_async_copy(src, dst, local.at[n])
        for n, (src, dst) in enumerate(
            [(r_hbm, r_ref), (l1_hbm, l1_ref), (l2_hbm, l2_ref), (d1_hbm, d1_ref), (d2_hbm, d2_ref)]
        )
    ]
    for copy in loads:
        copy.start()

    def remote(m, src, dst, device, arrival=None):
        return pltpu.make_async_remote_copy(
            src_ref=src,
            dst_ref=dst,
            send_sem=send.at[m],
            recv_sem=recv.at[m if arrival is None else arrival],
            device_id=device,
            device_id_type=MESH,
        )

    def push(m, src, dst, device, arrival=None):
        copy = remote(m, src, dst, device, arrival)
        copy.start()
        pending.append(copy)

    def arrive(m, dst):
        remote(m, dst, dst, sibling).wait_recv()

    s1 = seg1[q]
    s2 = seg2[q]
    parent = par2[s2]
    loads[1].wait()
    for a in range(2):
        m1 = pat1[s1, p + NB * a].astype(F32)
        g1[q, pl.ds(B * a, B)] = (l1_ref[pl.ds(B * a, B), :] * m1).T
    mb = (pat2[s2, 2 * NB + p] * (seg1[p] == parent).astype(jnp.int32)).astype(F32)
    loads[2].wait()
    own_b = (l2_ref[pl.ds(2 * B, B), :] * mb).T
    bz[p] = own_b
    pl.semaphore_wait(barrier, len(partners))

    def prepare_root():
        loads[0].wait()
        for a in range(2):
            gr[y, a] = r_ref[pl.ds(a, 2 * B, stride=2), :].T

    def prepare_rest():
        gbd[q, :B] = own_b
        for a in range(2):
            ma = (pat2[s2, p + NB * a] * pat1[parent, p + NB * a]).astype(F32)
            ew[:, pl.ds(B * a, B)] = (l2_ref[pl.ds(B * a, B), :] * ma).T
        loads[3].wait()
        gbd[q, B:] = d1_ref[...].T
        loads[4].wait()

    def gather_root():
        for n, step in enumerate(STEPS):
            push(M_ROOT + n, gr.at[y], gr.at[y], at(0, step))
        yield
        for n, step in enumerate(STEPS):
            arrive(M_ROOT + n, gr.at[(y + NY - step) % NY])

    def gather(g, base, cut=B):
        def slot(h, du, dv):
            dx, dy = (du, dv) if h == 0 else (dv, du)
            rows = pl.ds(0, cut) if h == 0 else pl.ds(cut, 2 * B - cut)
            return g.at[((y + dy) % NY) * NX + (x + dx) % NX, rows]

        def first(h, n):
            view = slot(h, 0, 0)
            step = STEPS[n]
            push(base + 15 * h + n, view, view, at(step, 0) if h == 0 else at(0, step))

        def second(h, i, n):
            view = slot(h, OFFSETS[i], 0)
            step = STEPS[n]
            push(base + 15 * h + 3 + 3 * i + n, view, view, at(0, step) if h == 0 else at(step, 0))

        def got_first(h, n):
            arrive(base + 15 * h + n, slot(h, 4 - STEPS[n], 0))

        def got_second(h, i, n):
            arrive(base + 15 * h + 3 + 3 * i + n, slot(h, OFFSETS[i], 4 - STEPS[n]))

        for n in range(3):
            first(0, n)
            second(1, 0, n)
        for n in range(3):
            first(1, n)
            second(0, 0, n)
        yield
        for n in range(3):
            for h in range(2):
                got_first(h, n)
                for m in range(3):
                    second(h, 1 + n, m)
        for n in range(3):
            got_second(1, 0, n)
        yield
        for n in range(3):
            got_second(0, 0, n)
        for i in range(1, 4):
            for n in range(3):
                for h in range(2):
                    got_second(h, i, n)

    def column():
        turns = (1, 7, 2, 6, 3, 5, 4)

        def slot(turn, core):
            return bz.at[2 * ((z + turn) % NZ) + core]

        for n, turn in enumerate(turns):
            device = (2 * ((z + turn) % NZ) + c, q)
            push(M_BZ + n, slot(0, c), slot(0, c), device)
        push(M_BZ + 7, slot(0, c), slot(0, c), sibling)
        yield
        for n, turn in enumerate(turns):
            arrive(M_BZ + n, slot(NZ - turn, c))
            push(M_BZ + 8 + n, slot(NZ - turn, c), slot(NZ - turn, c), sibling)
        yield
        arrive(M_BZ + 7, slot(0, 1 - c))
        for n, turn in enumerate(turns):
            arrive(M_BZ + 8 + n, slot(NZ - turn, 1 - c))

    def reduce(part, other, up, down, base):
        order = (4, -3, 3, -2, 2, -1, 1, 0)

        def there(off):
            return (z + off + NZ) % NZ

        for n, off in enumerate(order):
            push(base + n, part.at[1 - c, there(off)], other.at[there(off)], sibling)
        yield

        def own(n, i):
            d = there(order[n])
            if i == 0:
                arrive(base + n, other.at[d])
            return part[c, d, i] + other[d, i]

        def hop(n, t, i, buffer, m, device):
            total = own(n, i)
            if t > 0:
                arrive(m + 2 * (t - 1) + i, buffer.at[t - 1, i])
                total = total + buffer[t - 1, i]
            d = there(order[n])
            part[c, d, i] = total
            push(m + 2 * t + i, part.at[c, d, i], buffer.at[t, i], device)

        for t in range(4):
            for i in range(2):
                hop(2 * t, t, i, up, base + 8, z_up)
                if t < 3:
                    hop(2 * t + 1, t, i, down, base + 16, z_down)
            yield
        for i in range(2):
            total = own(7, i)
            arrive(base + 20 + i, down.at[2, i])
            total = total + down[2, i]
            arrive(base + 14 + i, up.at[3, i])
            part[c, z, i] = total + up[3, i]

    def reduce_panel(part, other, chain, base):
        UP, DOWN = 0, 2
        offsets = (4 - odd, 2 - 5 * odd, 3 * odd - 2, 0 - odd)
        rows = [((z + off + NZ) % NZ) // 2 for off in offsets]
        even_sent, odd_sent = [], []
        odd_chip = jnp.logical_not(lands)

        def wait_own(n):
            arrive(base + n, other.at[rows[n]])

        def own(n, i):
            return part[c, rows[n], i] + other[rows[n], i]

        def got(kind, i):
            arrive(base + 4 + 4 * kind + i, chain.at[kind, i])
            return chain[kind, i]

        def onward(sent, n, i, kind, total):
            part[c, rows[n], i] = total
            device = z_up if kind < DOWN else z_down
            copy = remote(
                base + 4 + 4 * kind + i, part.at[c, rows[n], i], chain.at[kind, i], device
            )
            copy.start()
            sent.append((base + 4 + 4 * kind + i, rows[n], i, kind))

        for n in range(4):
            push(base + n, part.at[1 - c, rows[n]], other.at[rows[n]], sibling)
        yield

        @pl.when(lands)
        def _():
            wait_own(0)
            for i in range(2):
                onward(even_sent, 0, i, UP, own(0, i))
                onward(even_sent, 0, i + 2, DOWN, own(0, i + 2))

        @pl.when(odd_chip)
        def _():
            wait_own(0)
            wait_own(1)
            for i in range(2):
                onward(odd_sent, 0, i + 2, UP, own(0, i + 2))
                onward(odd_sent, 1, i, DOWN, own(1, i))

        yield

        @pl.when(odd_chip)
        def _():
            for i in range(2):
                onward(odd_sent, 0, i, UP, own(0, i) + got(UP, i))
                onward(odd_sent, 1, i + 2, DOWN, own(1, i + 2) + got(DOWN, i + 2))

        @pl.when(lands)
        def _():
            wait_own(1)
            wait_own(2)
            for i in range(2):
                onward(even_sent, 1, i + 2, UP + 1, own(1, i + 2) + got(UP, i + 2))
                onward(even_sent, 2, i, DOWN + 1, own(2, i) + got(DOWN, i))

        yield

        @pl.when(odd_chip)
        def _():
            wait_own(2)
            wait_own(3)
            for i in range(2):
                onward(odd_sent, 2, i + 2, UP + 1, own(2, i + 2) + got(UP + 1, i + 2))
                onward(odd_sent, 3, i, DOWN + 1, own(3, i) + got(DOWN + 1, i))

        @pl.when(lands)
        def _():
            for i in range(2):
                onward(even_sent, 1, i, UP + 1, own(1, i) + got(UP, i))
                onward(even_sent, 2, i + 2, DOWN + 1, own(2, i + 2) + got(DOWN, i + 2))

        yield

        @pl.when(odd_chip)
        def _():
            for i in range(2):
                onward(odd_sent, 2, i, UP + 1, own(2, i) + got(UP + 1, i))
                onward(odd_sent, 3, i + 2, DOWN + 1, own(3, i + 2) + got(DOWN + 1, i + 2))

        yield

        @pl.when(lands)
        def _():
            wait_own(3)
            for i in range(4):
                part[c, rows[3], i] = own(3, i) + got(UP + 1, i) + got(DOWN + 1, i)

        def drain():
            for condition, sent in ((lands, even_sent), (odd_chip, odd_sent)):
                @pl.when(condition)
                def _():
                    for m, row, i, kind in sent:
                        remote(m, part.at[c, row, i], chain.at[kind, i], z_up).wait_send()

        drains.append(drain)

    core = x % 2
    keeps = lands & (c == core)

    def hand_over(part, yt, base):
        for step in (1, 3, 2):
            @pl.when(lands)
            def _():
                i = (x + step) % NX
                remote(
                    base + step, part.at[c, z // 2, i], yt.at[c], (2 * z + core, y * NX + i), base + c
                ).start()

        @pl.when(keeps)
        def _():
            yt[c] = part[c, z // 2, x]

        @pl.when(lands & (c != core))
        def _():
            remote(base, part.at[c, z // 2, x], yt.at[c], sibling, base + c).start()

    def handed_over(part, yt, base):
        @pl.when(lands)
        def _():
            for step in (1, 3, 2):
                i = (x + step) % NX
                remote(
                    base + step, part.at[c, z // 2, i], yt.at[c], (2 * z + core, y * NX + i), base + c
                ).wait_send()

        @pl.when(lands & (c != core))
        def _():
            remote(base, part.at[c, z // 2, x], yt.at[c], sibling, base + c).wait_send()

    def take(yt, base):
        arrive(base + 1 - c, yt.at[1 - c])

        @pl.when(jnp.logical_not(keeps))
        def _():
            arrive(base + c, yt.at[c])

        return right3(yt[...].reshape(2 * B, B))

    GROUP = 4

    def panel(g, i):
        rows = pl.ds(i * GROUP, GROUP)
        return jnp.concatenate(
            [g[rows, :B].reshape(GROUP * B, B), g[rows, B:].reshape(GROUP * B, B)], axis=1
        )

    def times_root(g, part):
        right = right3(
            jnp.concatenate(
                [
                    jnp.concatenate([g[y * NX + i, :B].T, g[y * NX + i, B:].T], axis=0)
                    for i in range(NX)
                ],
                axis=1,
            )
        )
        for a in range(2):
            out = dot(left3(gr[:, a].reshape(NY * B, 2 * B)), right)
            for i in range(NX):
                part[a, :, i] = out[:, B * i : B * i + B].reshape(NY, B, B)

    def store_halves(part, i, out):
        rows = pl.ds(i * 2, 2)
        blocks = out.reshape(2, 2, B, B)
        part[0, rows] = blocks[:, :, : B // 2]
        part[1, rows] = blocks[:, :, B // 2 :]

    def finish(part, w, base):
        push(base, part.at[c, z, 1 - c], w.at[c], sibling)
        w[c] = part[c, z, c]

    first, bcol, root = gather(g1, M_G1, 64), column(), gather_root()
    whole, bd = gather(ge, M_GE), gather(gbd, M_BD)
    next(first)
    next(bcol)
    prepare_root()
    next(first)
    next(root)
    prepare_rest()
    next(bcol)
    rounds(first, bcol)
    next(bd)

    @pl.loop(0, NB // GROUP)
    def _(i):
        left = jnp.concatenate([bz[i * GROUP + k] for k in range(GROUP)], axis=1)
        ew[...] -= dot(left3(left), right3(panel(g1, i)))

    ge[q, :B] = ew[:, :B]
    ge[q, B:] = ew[:, B:]
    next(whole)
    rounds(root)
    times_root(g1, p1)

    def first_level():
        yield from reduce_panel(p1, x1, ch1, M_Y1)
        hand_over(p1, yt1, M_T1)

    def second_level():
        yield from reduce_panel(p2, x2, ch2, M_Y2)
        hand_over(p2, yt2, M_T2)

    level_one, level_two = first_level(), second_level()
    next(level_one)
    next(level_one)
    next(level_one)
    next(whole)
    next(bd)
    times_root(ge, p2)
    next(level_two)
    next(level_two)
    rounds(level_one, level_two)
    rounds(bd, whole)

    def corner_step(k, acc):
        return acc + dot(left3(bz[k]), right3(gbd[k, B:]))

    u3 = right3(lax.fori_loop(0, NB, corner_step, jnp.zeros((B, B), F32)).T)
    y1 = take(yt1, M_T1)

    @pl.loop(0, NB // GROUP)
    def _(i):
        store_halves(pz1, i, dot(left3(panel(g1, i)), y1))

    last_one = reduce(pz1, xz1, upz1, dnz1, M_Z1)
    next(last_one)
    y3 = take(yt2, M_T2)

    @pl.loop(0, NB // GROUP)
    def _(i):
        out = dot(left3(panel(ge, i)), y3)
        out = out + dot(left3(gbd[pl.ds(i * GROUP, GROUP), :B].reshape(GROUP * B, B)), u3)
        store_halves(pz2, i, out)

    rounds(reduce(pz2, xz2, upz2, dnz2, M_Z2), last_one)

    finish(pz1, w1, M_F1)
    finish(pz2, w2, M_F2)
    arrive(M_F1, w1.at[1 - c])
    arrive(M_F2, w2.at[1 - c])
    same1 = (seg1[p] == seg1[q]).astype(F32)
    same2 = (seg2[p] == seg2[q]).astype(F32)
    o1_ref[...] = (d1_ref[...] + w1[...].reshape(B, B)) * same1
    o2_ref[...] = (d2_ref[...] + w2[...].reshape(B, B)) * same2

    for copy in pending:
        copy.wait_send()
    for drain in drains:
        drain()
    handed_over(p1, yt1, M_T1)
    handed_over(p2, yt2, M_T2)


def on_device(
    root_inverse, lower_one, lower_two, dinv_one, dinv_two,
    seg_one, seg_two, parent_two, pattern_one, pattern_two,
):
    vmem = pl.BlockSpec(memory_space=pltpu.VMEM)
    smem = pl.BlockSpec(memory_space=pltpu.SMEM)
    hbm = pl.BlockSpec(memory_space=pltpu.HBM)

    def buf(*shape):
        return pltpu.VMEM(shape, F32)

    panel_sum = [buf(2, NY, NX, B, B), buf(NY, NX, B, B), buf(4, NX, B, B)]
    half = B // 2
    block_sum = [
        buf(2, NZ, 2, half, B),
        buf(NZ, 2, half, B),
        buf(4, 2, half, B),
        buf(3, 2, half, B),
    ]

    outs = pl.pallas_call(
        kernel,
        out_shape=[jax.ShapeDtypeStruct((B, B), F32)] * 2,
        in_specs=[smem] * 5 + [hbm] * 5,
        out_specs=[vmem] * 2,
        scratch_shapes=[
            buf(4 * B, B),
            buf(2 * B, B),
            buf(3 * B, B),
            buf(B, B),
            buf(B, B),
            buf(NY, 2, B, 2 * B),
            buf(NB, 2 * B, B),
            buf(NB, 2 * B, B),
            buf(NB, 2 * B, B),
            buf(NB, B, B),
            *panel_sum,
            *panel_sum,
            *block_sum,
            *block_sum,
            buf(2, B, B),
            buf(2, B, B),
            buf(2, B // 2, B),
            buf(2, B // 2, B),
            buf(B, 2 * B),
            pltpu.SemaphoreType.DMA((M_ALL,)),
            pltpu.SemaphoreType.DMA((M_ALL,)),
            pltpu.SemaphoreType.DMA((5,)),
        ],
        compiler_params=pltpu.CompilerParams(
            collective_id=0, has_side_effects=True, vmem_limit_bytes=56 << 20
        ),
    )(
        seg_one, seg_two, parent_two, pattern_one, pattern_two,
        root_inverse.reshape(4 * B, B),
        lower_one.reshape(2 * B, B),
        lower_two.reshape(3 * B, B),
        dinv_one.reshape(B, B),
        dinv_two.reshape(B, B),
    )
    return tuple(out.reshape(1, 1, B, 1, 1, B) for out in outs)


def solution(mesh):
    blocks = P(None, "prow", None, None, "pcol", None)
    return jax.shard_map(
        on_device,
        mesh=mesh,
        in_specs=(blocks,) * 5 + (P(),) * 5,
        out_specs=(blocks,) * 2,
        check_vma=False,
    )
```
